128 devices in a mesh: gx: 4 (over y), gy: 8 (over z_lo, x), gz: 4 (over z_hi, core).
Axes of the slice: x: 4, y: 4, z: 4 (z_hi: 2, z_lo: 2; z = z_hi * 2 + z_lo), core: 2. Of those that a mesh axis runs over, the one named last changes fastest.
Arguments:
- solution: float32 [16, 64, 128, 512], P(None, 'gx', 'gy', 'gz'), may hold values from -6 to 6
- residual: float32 [16, 64, 128, 512], P(None, 'gx', 'gy', 'gz'), may hold values from -15 to 15, as said below
- direction: float32 [16, 64, 128, 512], P(None, 'gx', 'gy', 'gz'), may hold values from -13 to 13, as said below
- kappa_squared: float32 [64, 128, 512], P('gx', 'gy', 'gz'), may hold values from 0.02 to 0.2
- conductance: float32 [64, 128, 512], P('gx', 'gy', 'gz'), may hold values from 0.1 to 1
Outputs:
- new_solution: float32 [16, 64, 128, 512], P(None, 'gx', 'gy', 'gz')
- new_residual: float32 [16, 64, 128, 512], P(None, 'gx', 'gy', 'gz')
- new_direction: float32 [16, 64, 128, 512], P(None, 'gx', 'gy', 'gz')
The draws below stay inside these ranges and needn't reach their ends.
Inputs may be any that keep to these rules, and one draw needn't show every extreme that they name: residual is drawn with a part that is independent for each sample and each cell. direction is correlated with residual, sample by sample.
All inputs are finite; a program needn't handle non-finite values.
Results may differ from the reference program's by a relative error of at most 0.0003.
Values sent between devices are 32-bit elements; how exact they have to be, the bound alone decides.
No kernel may reach another device: no remote copies, remote signals or barrier semaphores. Data moves between devices by JAX's collectives and lax.ppermute only.
A program may use at most 128 MiB of HBM per device.

```python
import math
import jax
import jax.numpy as jnp
from jax import lax

K = 16
ITERS = 2
NX = 64
NY = 128
NZ = 512


def rough_field(key):
    noise_key = jax.random.fold_in(key, 11)
    positions = jnp.arange(NX, dtype=jnp.float32)
    ramp = (1.0 + 2.0 * positions / max(NX - 1, 1)).reshape(1, NX, 1, 1)
    base = jnp.clip(jax.random.normal(noise_key, (K, NX, NY, NZ), jnp.float32), -5.0, 5.0)
    return ramp * base


def draw_residual(key, part):
    return rough_field(key)


def draw_direction(key, part):
    noise_key = jax.random.fold_in(key, 23)
    extra = jnp.clip(jax.random.normal(noise_key, (K, NX, NY, NZ), jnp.float32), -5.0, 5.0)
    return 0.6 * rough_field(key) + 0.8 * extra


def shard_levels(rng, extent, pieces, low, high):
    def one(dim, parts):
        heights = jax.random.uniform(jax.random.fold_in(jax.random.fold_in(rng, 6), dim), (parts,), jnp.float32, low / len(pieces), high / len(pieces))
        return jnp.repeat(jnp.exp(heights), extent[dim] // parts).reshape((-1,) + (1,) * (len(extent) - dim - 1))

    level = one(*pieces[0])
    for cut in pieces[1:]:
        level = level * one(*cut)
    return level


def centred(key, extent, scale, limit, cuts=(), held_as=jnp.bfloat16):
    gain = shard_levels(key, extent, cuts, -0.22, 0.18) if cuts else 1.0
    drawn = jax.random.normal(key, extent, jnp.float32) * scale * gain
    return jnp.minimum(jnp.maximum(drawn, -limit), limit).astype(held_as)


def setup_inputs(seed: int = 0) -> dict:
    keys = jax.random.split(jax.random.key(seed), 6)
    solution = centred(keys[0], (K, NX, NY, NZ), 1.0, 6.0, ((1, 4), (2, 8), (3, 4)), jnp.float32)
    residual = draw_residual(jax.random.fold_in(keys[5], 71), 0)
    direction = draw_direction(jax.random.fold_in(keys[5], 71), 0)
    kappa_squared = jnp.clip(jnp.exp(math.log(0.2) - 2.3025851 * jax.random.uniform(keys[3], (NX, NY, NZ), jnp.float32) ** shard_levels(keys[3], (NX, NY, NZ), ((0, 4), (1, 8), (2, 4)), -0.2, 0.2)), 0.02, 0.2)
    conductance = jnp.clip(jnp.exp(math.log(1.0) - 2.3025851 * jax.random.uniform(keys[4], (NX, NY, NZ), jnp.float32) ** shard_levels(keys[4], (NX, NY, NZ), ((0, 4), (1, 8), (2, 4)), -0.2, 0.2)), 0.1, 1.0)
    return {"solution": solution, "residual": residual, "direction": direction, "kappa_squared": kappa_squared, "conductance": conductance}


def six_sides(array):
    return [array[..., 2:, 1:-1, 1:-1], array[..., :-2, 1:-1, 1:-1], array[..., 1:-1, 2:, 1:-1], array[..., 1:-1, :-2, 1:-1], array[..., 1:-1, 1:-1, 2:], array[..., 1:-1, 1:-1, :-2]]

def laplace(padded, kappa, conduct):
    centre = padded[..., 1:-1, 1:-1, 1:-1]
    conduct_mid = conduct[1:-1, 1:-1, 1:-1]
    total = kappa * centre
    for beside, face_dif in zip(six_sides(padded), six_sides(conduct)):
        total = total + 0.5 * (conduct_mid + face_dif) * (centre - beside)
    return total

def precision_apply(field, kappa, conduct_pad):
    middle = laplace(jnp.pad(field, 1), kappa, conduct_pad)
    return laplace(jnp.pad(middle, 1), kappa, conduct_pad)

def gram(first, second, count):
    return jnp.dot(first.reshape(first.shape[0], -1), second.reshape(second.shape[0], -1).T, precision=lax.Precision.HIGHEST) / count

def symmetric(matrix):
    return 0.5 * (matrix + matrix.T)

def spd_solve(matrix, right):
    factor = jnp.linalg.cholesky(matrix)
    inner = lax.linalg.triangular_solve(factor, right, left_side=True, lower=True)
    return lax.linalg.triangular_solve(factor, inner, left_side=True, lower=True, transpose_a=True)

def combine(matrix, fields):
    flat = fields.reshape(fields.shape[0], -1)
    return jnp.dot(matrix, flat, precision=lax.Precision.HIGHEST).reshape(fields.shape)

def reference(solution, residual, direction, kappa_squared, conductance):
    count = jnp.float32(NX * NY * NZ)
    conduct_pad = jnp.pad(conductance, 1)
    for iteration in range(ITERS):
        image = lax.map(lambda sample: precision_apply(sample, kappa_squared, conduct_pad), direction)
        curvature = symmetric(gram(direction, image, count))
        projected = gram(direction, residual, count)
        step_mat = spd_solve(curvature, projected)
        solution = solution + combine(step_mat.T, direction)
        residual = residual - combine(step_mat.T, image)
        correction = -spd_solve(curvature, gram(image, residual, count))
        fresh = residual + combine(correction.T, direction)
        factor = jnp.linalg.cholesky(symmetric(gram(fresh, fresh, count)))
        inverse = lax.linalg.triangular_solve(factor, jnp.eye(K, dtype=jnp.float32), left_side=True, lower=True)
        direction = combine(inverse, fresh)
    return (solution, residual, direction)
```

```python
import functools

import jax
import jax.numpy as jnp
from jax import lax
from jax.experimental import pallas as pl
from jax.experimental.pallas import tpu as pltpu
from jax.sharding import PartitionSpec as P

AXES = ("gx", "gy", "gz")
S = 16
NX, NY, NZ = 16, 16, 128
F32, BF16 = jnp.float32, jnp.bfloat16
VMEM = pl.BlockSpec(memory_space=pltpu.VMEM)
PARAMS = pltpu.CompilerParams(vmem_limit_bytes=56 << 20)


def lanes(shape):
    return lax.broadcasted_iota(jnp.int32, shape, len(shape) - 1)


def lane_roll(v, shift):
    return pltpu.roll(v, shift, v.ndim - 1)


def put_z_face(ref, row, acc, off, lane):
    moved = lane_roll(acc, off)
    ref[row] = jnp.where((lane >= off) & (lane < off + NY), moved, ref[row])


def enter_kernel(d_ref, r_ref, c_ref, out_ref, xl, xh, yl, yh, zl, zh):
    x = pl.program_id(0)
    lane = lanes((S, NZ))
    off = lax.rem(x, 8) * NY
    for f, ref in enumerate((d_ref, r_ref)):
        flat = ref.reshape(S * NY, NZ)
        accl = jnp.zeros((S, NZ), F32)
        acch = jnp.zeros((S, NZ), F32)
        for y in range(NY):
            v = flat[pl.ds(y, S, stride=NY), :]
            out_ref[f, 0, y] = v
            accl = jnp.where(lane == y, lane_roll(v, y) if y else v, accl)
            acch = jnp.where(lane == y, lane_roll(v, y + 1), acch)
            if y == 0:
                yl[f * NX + x] = v
            if y == NY - 1:
                yh[f * NX + x] = v
        put_z_face(zl, f * 2 + x // 8, accl, off, lane)
        put_z_face(zh, f * 2 + x // 8, acch, off, lane)

    cond = c_ref[0]
    yl[2 * NX, pl.ds(x, 1), :] = cond[0:1]
    yh[2 * NX, pl.ds(x, 1), :] = cond[NY - 1 : NY]
    zl[4] = jnp.where(lane == x, lane_roll(cond, x), zl[4])
    zh[4] = jnp.where(lane == x, lane_roll(cond, x + 1), zh[4])

    @pl.when(x == 0)
    def _():
        for f in range(2):
            for y in range(NY):
                xl[f * NY + y] = out_ref[f, 0, y]
        xl[2 * NY] = cond

    @pl.when(x == NX - 1)
    def _():
        for f in range(2):
            for y in range(NY):
                xh[f * NY + y] = out_ref[f, 0, y]
        xh[2 * NY] = cond


def enter(direction, residual, conductance):
    block = pl.BlockSpec((S, 1, NY, NZ), lambda x: (0, x, 0, 0))
    whole = lambda n: pl.BlockSpec((n, S, NZ), lambda x: (0, 0, 0))
    shape = lambda n: jax.ShapeDtypeStruct((n, S, NZ), F32)
    rows = (33, 33, 33, 33, 5, 5)
    return pl.pallas_call(
        enter_kernel,
        grid=(NX,),
        in_specs=[block, block, pl.BlockSpec((1, NY, NZ), lambda x: (x, 0, 0))],
        out_specs=[pl.BlockSpec((2, 1, NY, S, NZ), lambda x: (0, x, 0, 0, 0))] + [whole(n) for n in rows],
        out_shape=[jax.ShapeDtypeStruct((2, NX, NY, S, NZ), F32)] + [shape(n) for n in rows],
        name="enter",
    )(direction, residual, conductance)


def coef_kernel(flag, kappa, cond, xl, xh, yl, yh, zl, zh, out):
    lane = lanes((NY, NZ))
    sub = lax.broadcasted_iota(jnp.int32, (NY, NZ), 0)

    def per_x(x, _):
        c = cond[x]
        prev = jnp.where(x == 0, xl[2 * NY] * flag[0], cond[jnp.maximum(x - 1, 0)])
        nxt = jnp.where(x == NX - 1, xh[2 * NY] * flag[1], cond[jnp.minimum(x + 1, NX - 1)])
        ylo = yl[2 * NX, pl.ds(x, 1), :] * flag[2]
        yhi = yh[2 * NX, pl.ds(x, 1), :] * flag[3]
        ym = jnp.where(sub == 0, ylo, pltpu.roll(c, 1, 0))
        yp = jnp.where(sub == NY - 1, yhi, pltpu.roll(c, NY - 1, 0))
        zlo = lane_roll(zl[4], lax.rem(NZ - x, NZ)) * flag[4]
        zhi = lane_roll(zh[4], NZ - 1 - x) * flag[5]
        zm = jnp.where(lane == 0, zlo, lane_roll(c, 1))
        zp = jnp.where(lane == NZ - 1, zhi, lane_roll(c, NZ - 1))
        g = [0.5 * (c + n) for n in (prev, nxt, ym, yp, zm, zp)]
        out[0, x] = kappa[x] + ((g[0] + g[1]) + (g[2] + g[3]) + (g[4] + g[5]))
        out[1, x] = jnp.where(x == 0, g[0] * flag[0], g[0])
        out[2, x] = jnp.where(x == NX - 1, g[1] * flag[1], g[1])
        out[3, x] = jnp.where(sub == 0, g[2] * flag[2], g[2])
        out[4, x] = jnp.where(sub == NY - 1, g[3] * flag[3], g[3])
        out[5, x] = jnp.where(lane == 0, g[4] * flag[4], g[4])
        out[6, x] = jnp.where(lane == NZ - 1, g[5] * flag[5], g[5])
        return 0

    lax.fori_loop(0, NX, per_x, 0)


def coefs(flags, kappa, cond, halos):
    return pl.pallas_call(
        coef_kernel,
        in_specs=[pl.BlockSpec(memory_space=pltpu.SMEM)] + [VMEM] * 8,
        out_specs=VMEM,
        out_shape=jax.ShapeDtypeStruct((7, NX, NY, NZ), F32),
        compiler_params=PARAMS,
        name="coefs",
    )(flags, kappa, cond, *halos)


def stencil_kernel(nf, ne, field, xl, xh, yl, yh, zl, zh, coef, out, *faces):
    lane = lanes((S, NZ))
    first, last = lane == 0, lane == NZ - 1
    if ne:
        oxl, oxh, oyl, oyh, ozl, ozh = faces

    def per_x(x, edge):
        off = lax.rem(x, 8) * NY
        back = lax.rem(NZ - off, NZ)
        half = x // 8
        zlo = [lane_roll(zl[f * 2 + half], back) for f in range(nf)]
        zhi = [lane_roll(zh[f * 2 + half], back) for f in range(nf)]
        accl = [jnp.zeros((S, NZ), F32) for _ in range(ne)]
        acch = [jnp.zeros((S, NZ), F32) for _ in range(ne)]
        for y in range(NY):
            k = [jnp.broadcast_to(coef[i, x, y : y + 1, :], (S, NZ)) for i in range(7)]
            for f in range(nf):
                c = field[f, x, y]
                xm = xl[f * NY + y] if edge == "lo" else field[f, x - 1, y]
                xp = xh[f * NY + y] if edge == "hi" else field[f, x + 1, y]
                ym = field[f, x, y - 1] if y else yl[f * NX + x]
                yp = field[f, x, y + 1] if y < NY - 1 else yh[f * NX + x]
                zm = jnp.where(first, lane_roll(zlo[f], (NZ - y) % NZ) if y else zlo[f], lane_roll(c, 1))
                zp = jnp.where(last, lane_roll(zhi[f], NZ - 1 - y), lane_roll(c, NZ - 1))
                o = ((k[0] * c - k[1] * xm) - (k[2] * xp + k[3] * ym)) - ((k[4] * yp + k[5] * zm) + k[6] * zp)
                out[f, x, y] = o
                if f < ne:
                    accl[f] = jnp.where(lane == y, lane_roll(o, y) if y else o, accl[f])
                    acch[f] = jnp.where(lane == y, lane_roll(o, y + 1), acch[f])
                    if edge == "lo":
                        oxl[f * NY + y] = o
                    if edge == "hi":
                        oxh[f * NY + y] = o
                    if y == 0:
                        oyl[f * NX + x] = o
                    if y == NY - 1:
                        oyh[f * NX + x] = o
        for f in range(ne):
            put_z_face(ozl, f * 2 + half, accl[f], off, lane)
            put_z_face(ozh, f * 2 + half, acch[f], off, lane)

    per_x(jnp.int32(0), "lo")
    lax.fori_loop(1, NX - 1, lambda x, c: (per_x(x, ""), c)[1], 0)
    per_x(jnp.int32(NX - 1), "hi")


def stencil(field, halos, coef, nf, ne):
    shape = lambda n: jax.ShapeDtypeStruct((n, S, NZ), F32)
    faces = [shape(n) for n in (16 * ne, 16 * ne, 16 * ne, 16 * ne, 2 * ne, 2 * ne)] if ne else []
    return pl.pallas_call(
        functools.partial(stencil_kernel, nf, ne),
        in_specs=[VMEM] * 8,
        out_specs=[VMEM] * (1 + len(faces)),
        out_shape=[jax.ShapeDtypeStruct((nf, NX, NY, S, NZ), F32)] + faces,
        compiler_params=PARAMS,
        name=f"stencil{nf}{ne}",
    )(field, *halos, coef)


def exchange(faces):
    halos = []
    for i, axis in enumerate(AXES):
        n = lax.axis_size(axis)
        low, high = faces[2 * i], faces[2 * i + 1]
        halos.append(lax.ppermute(high, axis, [(j, (j + 1) % n) for j in range(n)]))
        halos.append(lax.ppermute(low, axis, [(j, (j - 1) % n) for j in range(n)]))
    return halos


def gram_kernel(dr, qw, z, halves, gram, acc):
    x = pl.program_id(0)
    fields = (dr.at[0, 0], qw.at[0, 0], dr.at[1, 0], qw.at[1, 0], z.at[0, 0])
    for y in range(NY):
        for i, ref in enumerate(fields):
            v = ref[y]
            hi = v.astype(BF16)
            halves[y, 16 * i : 16 * i + 16, :] = hi
            halves[y, 80 + 16 * i : 96 + 16 * i, :] = (v - hi.astype(F32)).astype(BF16)
    op = jnp.concatenate([halves[y] for y in range(NY)], axis=1)
    part = lax.dot_general(op, op, (((1,), (1,)), ((), ())), preferred_element_type=F32)

    @pl.when(x == 0)
    def _():
        acc[...] = part

    @pl.when(x > 0)
    def _():
        acc[...] = acc[...] + part

    @pl.when(x == NX - 1)
    def _():
        a = acc[...]
        rows = a[:80] + a[80:]
        left, right = rows[:, :128], jnp.concatenate([rows[:, 128:], jnp.zeros((80, 96), F32)], axis=1)
        lane = lanes((80, 128))
        second = jnp.where(lane < 48, lane_roll(left, 48), lane_roll(right, 48))
        gram[...] = jnp.where(lane < 80, left + second, 0.0)


def gram(dr, qw, z):
    two = pl.BlockSpec((2, 1, NY, S, NZ), lambda x: (0, x, 0, 0, 0))
    one = pl.BlockSpec((1, 1, NY, S, NZ), lambda x: (0, x, 0, 0, 0))
    return pl.pallas_call(
        gram_kernel,
        grid=(NX,),
        in_specs=[two, two, one],
        out_specs=[pl.BlockSpec((NY, 160, NZ), lambda x: (x, 0, 0)), pl.BlockSpec((80, 128), lambda x: (0, 0))],
        out_shape=[jax.ShapeDtypeStruct((NX * NY, 160, NZ), BF16), jax.ShapeDtypeStruct((80, 128), F32)],
        scratch_shapes=[pltpu.VMEM((160, 160), F32)],
        name="gram",
    )(dr, qw, z)


def reduce_all(part):
    for axis in ("gx", "gz"):
        n = lax.axis_size(axis)
        part = part + sum(lax.ppermute(part, axis, [(j, j ^ s) for j in range(n)]) for s in range(1, n))
    n = lax.axis_size("gy")
    spread = jnp.broadcast_to(part[None], (n,) + part.shape)
    return lax.all_to_all(spread, "gy", 0, 0, tiled=True).sum(0)


def rows128(m):
    return jnp.concatenate([m, jnp.zeros((128 - m.shape[0], 128), F32)], axis=0)


def mm(a, b):
    return jnp.dot(a, rows128(b), precision=lax.Precision.HIGHEST, preferred_element_type=F32)


def mm_nt(a, b):
    return lax.dot_general(
        a, rows128(b), (((1,), (1,)), ((), ())), precision=lax.Precision.HIGHEST, preferred_element_type=F32
    )


def eye_at(lane, sub, off):
    return jnp.where(lane == sub + off, 1.0, 0.0).astype(F32)


def spd_inverse(m, lane, sub):
    m = jnp.where(lane < 16, m, eye_at(lane, sub, 16))
    for k in range(S):
        row = m[k : k + 1, :]
        row = row / row[:, k : k + 1]
        m = jnp.where(sub == k, row, m - m[:, k : k + 1] * row)
    return jnp.where(lane < 16, lane_roll(m, 112), 0.0)


def factor_inverse(m, lane, sub):
    m = jnp.where(lane < 16, m, eye_at(lane, sub, 16))
    for k in range(S):
        row = m[k : k + 1, :]
        scale = lax.rsqrt(row[:, k : k + 1])
        row = row * scale
        m = jnp.where(sub == k, row, jnp.where(sub > k, m - (m[:, k : k + 1] * scale) * row, m))
    return jnp.where(lane < 16, lane_roll(m, 112), 0.0)


def step(g, lane, sub):
    gd, gq, gr = g[:16], g[16:32], g[32:48]
    low = lane < 16
    curvature = 0.5 * (lane_roll(gd, 112) + gq)
    inv = spd_inverse(curvature, lane, sub)
    s_t = mm(jnp.where(low, gr, 0.0), inv)
    qq = jnp.where(low, lane_roll(gq, 112), 0.0)
    rq = jnp.where(low, lane_roll(gr, 112), 0.0) - mm(s_t, qq)
    c_t = -mm(rq, inv)
    r_t = eye_at(lane, sub, 32) - lane_roll(s_t, 16)
    f_t = r_t + c_t
    ff = mm_nt(mm(f_t, g), f_t)
    ff = 0.5 * (ff + mm_nt(f_t, mm(f_t, g)))
    inv_factor = factor_inverse(ff, lane, sub)
    return s_t, r_t, mm(inv_factor, f_t)


def algebra_kernel(gram_ref, coef_ref):
    lane = lanes((S, 128))
    sub = lax.broadcasted_iota(jnp.int32, (S, 128), 0)
    g = gram_ref[...] * (1.0 / (64 * 128 * 512))
    lane48 = lanes((48, 128))
    g1 = jnp.where(lane48 < 48, g[:48], 0.0)
    s_t, r_t, d_t = step(g1, lane, sub)
    q_t = (
        lane_roll(jnp.where(lane < 16, d_t, 0.0), 16)
        + lane_roll(jnp.where((lane >= 32) & (lane < 48), d_t, 0.0), 16)
        + lane_roll(jnp.where((lane >= 16) & (lane < 32), d_t, 0.0), 48)
    )
    t = jnp.concatenate([d_t, q_t, r_t], axis=0)
    g2 = mm_nt(mm(t, g), t)
    s2_t, r2_t, d2_t = step(g2, lane, sub)
    final = mm(jnp.concatenate([s2_t, r2_t, d2_t], axis=0), t)
    final = jnp.concatenate([final[:16] + s_t, final[16:]], axis=0)
    hi = final.astype(BF16).astype(F32)
    for i, part in enumerate((hi, final - hi)):
        twice = lane_roll(part, 80)
        coef_ref[48 * i : 48 * i + 48, :128] = jnp.where(lane48 < 80, part, twice).astype(BF16)
        coef_ref[48 * i : 48 * i + 48, 128:] = jnp.where(lane48 < 32, twice, 0.0).astype(BF16)


def algebra(total):
    return pl.pallas_call(
        algebra_kernel,
        in_specs=[VMEM],
        out_specs=VMEM,
        out_shape=jax.ShapeDtypeStruct((96, 256), BF16),
        name="algebra",
    )(total)


def leave_kernel(coef, halves, sol, xo, ro, do):
    left = coef[:, :160]
    flat = [ref.reshape(S * NY, NZ) for ref in (xo, ro, do)]
    inp = sol.reshape(S * NY, NZ)
    for y in range(0, NY, 2):
        pair = jnp.concatenate([halves[y], halves[y + 1]], axis=1)
        res = jnp.dot(left, pair, preferred_element_type=F32)
        res = res[:48] + res[48:]
        for j in range(2):
            v = res[:, j * NZ : (j + 1) * NZ]
            rows = pl.ds(y + j, S, stride=NY)
            flat[0][rows, :] = inp[rows, :] + v[:16]
            flat[1][rows, :] = v[16:32]
            flat[2][rows, :] = v[32:48]


def leave(coef, halves, sol):
    block = pl.BlockSpec((S, 1, NY, NZ), lambda x: (0, x, 0, 0))
    return pl.pallas_call(
        leave_kernel,
        grid=(NX,),
        in_specs=[pl.BlockSpec((96, 256), lambda x: (0, 0)), pl.BlockSpec((NY, 160, NZ), lambda x: (x, 0, 0)), block],
        out_specs=[block] * 3,
        out_shape=[jax.ShapeDtypeStruct((S, NX, NY, NZ), F32)] * 3,
        name="leave",
    )(coef, halves, sol)


def edge_flags():
    vals = []
    for axis in AXES:
        i, n = lax.axis_index(axis), lax.axis_size(axis)
        vals += [i > 0, i < n - 1]
    return jnp.stack(vals).astype(F32)


def body(sol, residual, direction, kappa, cond):
    dr, *faces = enter(direction, residual, cond)
    halos = exchange(faces)
    coef = coefs(edge_flags(), kappa, cond, halos)
    mid, *faces = stencil(dr, halos, coef, 2, 2)
    qw, *faces = stencil(mid, exchange(faces), coef, 2, 1)
    mid, *faces = stencil(qw, exchange(faces), coef, 1, 1)
    (z,) = stencil(mid, exchange(faces), coef, 1, 0)
    halves, part = gram(dr, qw, z)
    return tuple(leave(algebra(reduce_all(part)), halves, sol))


def solution(mesh):
    fields = P(None, *AXES)
    cells = P(*AXES)
    return jax.shard_map(
        body,
        mesh=mesh,
        in_specs=(fields, fields, fields, cells, cells),
        out_specs=(fields, fields, fields),
        check_vma=False,
    )
```

```python
import functools

import jax
import jax.numpy as jnp
from jax import lax
from jax.experimental import pallas as pl
from jax.experimental.pallas import tpu as pltpu
from jax.sharding import PartitionSpec as P

AXES = ("gx", "gy", "gz")
S = 16
NX, NY, NZ = 16, 16, 128
F32, BF16 = jnp.float32, jnp.bfloat16
VMEM = pl.BlockSpec(memory_space=pltpu.VMEM)


def grant(mib):
    return pltpu.CompilerParams(vmem_limit_bytes=mib << 20)


def lanes(shape):
    return lax.broadcasted_iota(jnp.int32, shape, len(shape) - 1)


def lane_roll(v, shift):
    return pltpu.roll(v, shift, v.ndim - 1)


def pack_z(acc, v, y, lane):
    return jnp.where((lane == 2 * y) | (lane == 2 * y + 1), lane_roll(v, 2 * y + 1), acc)


def put_z_face(ref, row, acc, off, lane):
    moved = lane_roll(acc, off)
    ref[row] = jnp.where((lane >= off) & (lane < off + 2 * NY), moved, ref[row])


def enter_kernel(d_ref, r_ref, c_ref, out_ref, xl, xh, yl, yh, zf):
    x = pl.program_id(0)
    lane = lanes((S, NZ))
    off = lax.rem(x, 4) * 32
    for f, ref in enumerate((d_ref, r_ref)):
        flat = ref.reshape(S * NY, NZ)
        acc = jnp.zeros((S, NZ), F32)
        for y in range(NY):
            v = flat[pl.ds(y, S, stride=NY), :]
            out_ref[f, 0, y] = v
            acc = pack_z(acc, v, y, lane)
            if y == 0:
                yl[f * NX + x] = v
            if y == NY - 1:
                yh[f * NX + x] = v
        put_z_face(zf, f * 4 + x // 4, acc, off, lane)

    cond = c_ref[0]
    yl[2 * NX, pl.ds(x, 1), :] = cond[0:1]
    yh[2 * NX, pl.ds(x, 1), :] = cond[NY - 1 : NY]
    zf[8] = jnp.where((lane == 2 * x) | (lane == 2 * x + 1), lane_roll(cond, 2 * x + 1), zf[8])

    @pl.when(x == 0)
    def _():
        for f in range(2):
            for y in range(NY):
                xl[f * NY + y] = out_ref[f, 0, y]
        xl[2 * NY] = cond

    @pl.when(x == NX - 1)
    def _():
        for f in range(2):
            for y in range(NY):
                xh[f * NY + y] = out_ref[f, 0, y]
        xh[2 * NY] = cond


def enter(direction, residual, conductance):
    block = pl.BlockSpec((S, 1, NY, NZ), lambda x: (0, x, 0, 0))
    whole = lambda n: pl.BlockSpec((n, S, NZ), lambda x: (0, 0, 0))
    shape = lambda n: jax.ShapeDtypeStruct((n, S, NZ), F32)
    rows = (33, 33, 33, 33, 9)
    return pl.pallas_call(
        enter_kernel,
        grid=(NX,),
        in_specs=[block, block, pl.BlockSpec((1, NY, NZ), lambda x: (x, 0, 0))],
        out_specs=[pl.BlockSpec((2, 1, NY, S, NZ), lambda x: (0, x, 0, 0, 0))] + [whole(n) for n in rows],
        out_shape=[jax.ShapeDtypeStruct((2, NX, NY, S, NZ), F32)] + [shape(n) for n in rows],
        compiler_params=grant(4),
        name="enter",
    )(direction, residual, conductance)


def coef_kernel(flag, kappa, cond, xl, xh, yl, yh, zl, zh, out):
    lane = lanes((NY, NZ))
    sub = lax.broadcasted_iota(jnp.int32, (NY, NZ), 0)

    def per_x(x, _):
        c = cond[x]
        prev = jnp.where(x == 0, xl[2 * NY] * flag[0], cond[jnp.maximum(x - 1, 0)])
        nxt = jnp.where(x == NX - 1, xh[2 * NY] * flag[1], cond[jnp.minimum(x + 1, NX - 1)])
        ylo = yl[2 * NX, pl.ds(x, 1), :] * flag[2]
        yhi = yh[2 * NX, pl.ds(x, 1), :] * flag[3]
        ym = jnp.where(sub == 0, ylo, pltpu.roll(c, 1, 0))
        yp = jnp.where(sub == NY - 1, yhi, pltpu.roll(c, NY - 1, 0))
        zlo = lane_roll(zl[8], lax.rem(NZ - 2 * x, NZ)) * flag[4]
        zhi = lane_roll(zh[8], NZ - 2 - 2 * x) * flag[5]
        zm = jnp.where(lane == 0, zlo, lane_roll(c, 1))
        zp = jnp.where(lane == NZ - 1, zhi, lane_roll(c, NZ - 1))
        g = [0.5 * (c + n) for n in (prev, nxt, ym, yp, zm, zp)]
        out[0, x] = kappa[x] + ((g[0] + g[1]) + (g[2] + g[3]) + (g[4] + g[5]))
        out[1, x] = jnp.where(x == 0, g[0] * flag[0], g[0])
        out[2, x] = jnp.where(x == NX - 1, g[1] * flag[1], g[1])
        out[3, x] = jnp.where(sub == 0, g[2] * flag[2], g[2])
        out[4, x] = jnp.where(sub == NY - 1, g[3] * flag[3], g[3])
        out[5, x] = jnp.where(lane == 0, g[4] * flag[4], g[4])
        out[6, x] = jnp.where(lane == NZ - 1, g[5] * flag[5], g[5])
        return 0

    lax.fori_loop(0, NX, per_x, 0)


def coefs(flags, kappa, cond, halos):
    return pl.pallas_call(
        coef_kernel,
        in_specs=[pl.BlockSpec(memory_space=pltpu.SMEM)] + [VMEM] * 8,
        out_specs=VMEM,
        out_shape=jax.ShapeDtypeStruct((7, NX, NY, NZ), F32),
        compiler_params=grant(4),
        name="coefs",
    )(flags, kappa, cond, *halos)


def stencil_kernel(nf, ne, field, xl, xh, yl, yh, zl, zh, coef, out, *faces):
    lane = lanes((S, NZ))
    first, last = lane == 0, lane == NZ - 1
    even = lax.rem(lane, 2) == 0
    if ne:
        oxl, oxh, oyl, oyh, ozf = faces

    def per_x(x, edge):
        off = lax.rem(x, 4) * 32
        quarter = x // 4
        for f in range(nf):
            beyond = jnp.where(even, lane_roll(zl[f * 4 + quarter], 2), zh[f * 4 + quarter])
            beyond = lane_roll(beyond, lax.rem(NZ - off, NZ))
            acc = jnp.zeros((S, NZ), F32)
            for y in range(NY):
                k = [jnp.broadcast_to(coef[i, x, y : y + 1, :], (S, NZ)) for i in range(7)]
                c = field[f, x, y]
                xm = xl[f * NY + y] if edge == "lo" else field[f, x - 1, y]
                xp = xh[f * NY + y] if edge == "hi" else field[f, x + 1, y]
                ym = field[f, x, y - 1] if y else yl[f * NX + x]
                yp = field[f, x, y + 1] if y < NY - 1 else yh[f * NX + x]
                ends = lane_roll(beyond, NZ - 2 - 2 * y)
                zm = jnp.where(first, ends, lane_roll(c, 1))
                zp = jnp.where(last, ends, lane_roll(c, NZ - 1))
                o = ((k[0] * c - k[1] * xm) - (k[2] * xp + k[3] * ym)) - ((k[4] * yp + k[5] * zm) + k[6] * zp)
                out[f, x, y] = o
                if f < ne:
                    acc = pack_z(acc, o, y, lane)
                    if edge == "lo":
                        oxl[f * NY + y] = o
                    if edge == "hi":
                        oxh[f * NY + y] = o
                    if y == 0:
                        oyl[f * NX + x] = o
                    if y == NY - 1:
                        oyh[f * NX + x] = o
            if f < ne:
                put_z_face(ozf, f * 4 + quarter, acc, off, lane)

    per_x(jnp.int32(0), "lo")
    lax.fori_loop(1, NX - 1, lambda x, c: (per_x(x, ""), c)[1], 0)
    per_x(jnp.int32(NX - 1), "hi")


def stencil(field, halos, coef, nf, ne):
    shape = lambda n: jax.ShapeDtypeStruct((n, S, NZ), F32)
    faces = [shape(n) for n in (16 * ne, 16 * ne, 16 * ne, 16 * ne, 4 * ne)] if ne else []
    return pl.pallas_call(
        functools.partial(stencil_kernel, nf, ne),
        in_specs=[VMEM] * 8,
        out_specs=[VMEM] * (1 + len(faces)),
        out_shape=[jax.ShapeDtypeStruct((nf, NX, NY, S, NZ), F32)] + faces,
        compiler_params=grant(6 * nf + 3),
        name=f"stencil{nf}{ne}",
    )(field, *halos, coef)


def exchange(faces):
    xl, xh, yl, yh, zf = faces
    halos = []
    for axis, low, high in (("gx", xl, xh), ("gy", yl, yh), ("gz", zf, zf)):
        n = lax.axis_size(axis)
        halos.append(lax.ppermute(high, axis, [(j, (j + 1) % n) for j in range(n)]))
        halos.append(lax.ppermute(low, axis, [(j, (j - 1) % n) for j in range(n)]))
    return halos


def gram_kernel(dr, qw, z, halves, gram, acc):
    x = pl.program_id(0)
    fields = (dr.at[0, 0], qw.at[0, 0], dr.at[1, 0], qw.at[1, 0], z.at[0, 0])
    for y in range(NY):
        for i, ref in enumerate(fields):
            v = ref[y]
            hi = v.astype(BF16)
            halves[y, 16 * i : 16 * i + 16, :] = hi
            halves[y, 80 + 16 * i : 96 + 16 * i, :] = (v - hi.astype(F32)).astype(BF16)
    op = jnp.concatenate([halves[y] for y in range(NY)], axis=1)
    part = lax.dot_general(op, op, (((1,), (1,)), ((), ())), preferred_element_type=F32)

    @pl.when(x == 0)
    def _():
        acc[...] = part

    @pl.when(x > 0)
    def _():
        acc[...] = acc[...] + part

    @pl.when(x == NX - 1)
    def _():
        a = acc[...]
        rows = a[:80] + a[80:]
        left, right = rows[:, :128], jnp.concatenate([rows[:, 128:], jnp.zeros((80, 96), F32)], axis=1)
        lane = lanes((80, 128))
        second = jnp.where(lane < 48, lane_roll(left, 48), lane_roll(right, 48))
        gram[...] = jnp.where(lane < 80, left + second, 0.0)


def gram(dr, qw, z):
    two = pl.BlockSpec((2, 1, NY, S, NZ), lambda x: (0, x, 0, 0, 0))
    one = pl.BlockSpec((1, 1, NY, S, NZ), lambda x: (0, x, 0, 0, 0))
    return pl.pallas_call(
        gram_kernel,
        grid=(NX,),
        in_specs=[two, two, one],
        out_specs=[pl.BlockSpec((NY, 160, NZ), lambda x: (x, 0, 0)), pl.BlockSpec((80, 128), lambda x: (0, 0))],
        out_shape=[jax.ShapeDtypeStruct((NX * NY, 160, NZ), BF16), jax.ShapeDtypeStruct((80, 128), F32)],
        scratch_shapes=[pltpu.VMEM((160, 160), F32)],
        compiler_params=grant(5),
        name="gram",
    )(dr, qw, z)


def reduce_all(part):
    for axis in ("gx", "gz"):
        n = lax.axis_size(axis)
        part = part + sum(lax.ppermute(part, axis, [(j, j ^ s) for j in range(n)]) for s in range(1, n))
    n = lax.axis_size("gy")
    spread = jnp.broadcast_to(part[None], (n,) + part.shape)
    return lax.all_to_all(spread, "gy", 0, 0, tiled=True).sum(0)


def rows128(m):
    return jnp.concatenate([m, jnp.zeros((128 - m.shape[0], 128), F32)], axis=0)


def mm(a, b):
    return jnp.dot(a, rows128(b), precision=lax.Precision.HIGHEST, preferred_element_type=F32)


def mm_nt(a, b):
    return lax.dot_general(
        a, rows128(b), (((1,), (1,)), ((), ())), precision=lax.Precision.HIGHEST, preferred_element_type=F32
    )


def eye_at(lane, sub, off):
    return jnp.where(lane == sub + off, 1.0, 0.0).astype(F32)


def spd_inverse(m, lane, sub):
    m = jnp.where(lane < 16, m, eye_at(lane, sub, 16))
    for k in range(S):
        row = m[k : k + 1, :]
        row = row / row[:, k : k + 1]
        m = jnp.where(sub == k, row, m - m[:, k : k + 1] * row)
    return jnp.where(lane < 16, lane_roll(m, 112), 0.0)


def factor_inverse(m, lane, sub):
    m = jnp.where(lane < 16, m, eye_at(lane, sub, 16))
    for k in range(S):
        row = m[k : k + 1, :]
        scale = lax.rsqrt(row[:, k : k + 1])
        row = row * scale
        m = jnp.where(sub == k, row, jnp.where(sub > k, m - (m[:, k : k + 1] * scale) * row, m))
    return jnp.where(lane < 16, lane_roll(m, 112), 0.0)


def step(g, lane, sub):
    gd, gq, gr = g[:16], g[16:32], g[32:48]
    low = lane < 16
    curvature = 0.5 * (lane_roll(gd, 112) + gq)
    inv = spd_inverse(curvature, lane, sub)
    s_t = mm(jnp.where(low, gr, 0.0), inv)
    qq = jnp.where(low, lane_roll(gq, 112), 0.0)
    rq = jnp.where(low, lane_roll(gr, 112), 0.0) - mm(s_t, qq)
    c_t = -mm(rq, inv)
    r_t = eye_at(lane, sub, 32) - lane_roll(s_t, 16)
    f_t = r_t + c_t
    ff = mm_nt(mm(f_t, g), f_t)
    ff = 0.5 * (ff + mm_nt(f_t, mm(f_t, g)))
    inv_factor = factor_inverse(ff, lane, sub)
    return s_t, r_t, mm(inv_factor, f_t)


def algebra_kernel(gram_ref, coef_ref):
    lane = lanes((S, 128))
    sub = lax.broadcasted_iota(jnp.int32, (S, 128), 0)
    g = gram_ref[...] * (1.0 / (64 * 128 * 512))
    lane48 = lanes((48, 128))
    g1 = jnp.where(lane48 < 48, g[:48], 0.0)
    s_t, r_t, d_t = step(g1, lane, sub)
    q_t = (
        lane_roll(jnp.where(lane < 16, d_t, 0.0), 16)
        + lane_roll(jnp.where((lane >= 32) & (lane < 48), d_t, 0.0), 16)
        + lane_roll(jnp.where((lane >= 16) & (lane < 32), d_t, 0.0), 48)
    )
    t = jnp.concatenate([d_t, q_t, r_t], axis=0)
    g2 = mm_nt(mm(t, g), t)
    s2_t, r2_t, d2_t = step(g2, lane, sub)
    final = mm(jnp.concatenate([s2_t, r2_t, d2_t], axis=0), t)
    final = jnp.concatenate([final[:16] + s_t, final[16:]], axis=0)
    hi = final.astype(BF16).astype(F32)
    for i, part in enumerate((hi, final - hi)):
        twice = lane_roll(part, 80)
        coef_ref[48 * i : 48 * i + 48, :128] = jnp.where(lane48 < 80, part, twice).astype(BF16)
        coef_ref[48 * i : 48 * i + 48, 128:] = jnp.where(lane48 < 32, twice, 0.0).astype(BF16)


def algebra(total):
    return pl.pallas_call(
        algebra_kernel,
        in_specs=[VMEM],
        out_specs=VMEM,
        out_shape=jax.ShapeDtypeStruct((96, 256), BF16),
        compiler_params=grant(2),
        name="algebra",
    )(total)


def leave_kernel(coef, halves, sol, xo, ro, do):
    left = coef[:, :160]
    flat = [ref.reshape(S * NY, NZ) for ref in (xo, ro, do)]
    inp = sol.reshape(S * NY, NZ)
    for y in range(0, NY, 2):
        pair = jnp.concatenate([halves[y], halves[y + 1]], axis=1)
        res = jnp.dot(left, pair, preferred_element_type=F32)
        res = res[:48] + res[48:]
        for j in range(2):
            v = res[:, j * NZ : (j + 1) * NZ]
            rows = pl.ds(y + j, S, stride=NY)
            flat[0][rows, :] = inp[rows, :] + v[:16]
            flat[1][rows, :] = v[16:32]
            flat[2][rows, :] = v[32:48]


def leave(coef, halves, sol):
    block = pl.BlockSpec((S, 1, NY, NZ), lambda x: (0, x, 0, 0))
    return pl.pallas_call(
        leave_kernel,
        grid=(NX,),
        in_specs=[pl.BlockSpec((96, 256), lambda x: (0, 0)), pl.BlockSpec((NY, 160, NZ), lambda x: (x, 0, 0)), block],
        out_specs=[block] * 3,
        out_shape=[jax.ShapeDtypeStruct((S, NX, NY, NZ), F32)] * 3,
        compiler_params=grant(8),
        name="leave",
    )(coef, halves, sol)


def edge_flags():
    vals = []
    for axis in AXES:
        i, n = lax.axis_index(axis), lax.axis_size(axis)
        vals += [i > 0, i < n - 1]
    return jnp.stack(vals).astype(F32)


def body(sol, residual, direction, kappa, cond):
    dr, *faces = enter(direction, residual, cond)
    halos = exchange(faces)
    coef = coefs(edge_flags(), kappa, cond, halos)
    mid, *faces = stencil(dr, halos, coef, 2, 2)
    qw, *faces = stencil(mid, exchange(faces), coef, 2, 1)
    mid, *faces = stencil(qw, exchange(faces), coef, 1, 1)
    (z,) = stencil(mid, exchange(faces), coef, 1, 0)
    halves, part = gram(dr, qw, z)
    return tuple(leave(algebra(reduce_all(part)), halves, sol))


def solution(mesh):
    fields = P(None, *AXES)
    cells = P(*AXES)
    return jax.shard_map(
        body,
        mesh=mesh,
        in_specs=(fields, fields, fields, cells, cells),
        out_specs=(fields, fields, fields),
        check_vma=False,
    )
```

```python
import functools

import jax
import jax.numpy as jnp
from jax import lax
from jax.experimental import pallas as pl
from jax.experimental.pallas import tpu as pltpu
from jax.sharding import PartitionSpec as P

AXES = ("gx", "gy", "gz")
S = 16
NX, NY, NZ = 16, 16, 128
F32, BF16 = jnp.float32, jnp.bfloat16
VMEM = pl.BlockSpec(memory_space=pltpu.VMEM)


def grant(mib):
    return pltpu.CompilerParams(vmem_limit_bytes=mib << 20)


def lanes(shape):
    return lax.broadcasted_iota(jnp.int32, shape, len(shape) - 1)


def lane_roll(v, shift):
    return pltpu.roll(v, shift, v.ndim - 1)


def pack_z(acc, v, y, lane):
    return jnp.where((lane == 2 * y) | (lane == 2 * y + 1), lane_roll(v, 2 * y + 1), acc)


def put_z_face(ref, row, acc, off, lane):
    moved = lane_roll(acc, off)
    ref[row] = jnp.where((lane >= off) & (lane < off + 2 * NY), moved, ref[row])


def enter_kernel(d_ref, r_ref, c_ref, d_out, r_out, xl, xh, yl, yh, zf):
    x = pl.program_id(0)
    lane = lanes((S, NZ))
    off = lax.rem(x, 4) * 32
    outs = (d_out, r_out)
    for f, ref in enumerate((d_ref, r_ref)):
        flat = ref.reshape(S * NY, NZ)
        acc = jnp.zeros((S, NZ), F32)
        for y in range(NY):
            v = flat[pl.ds(y, S, stride=NY), :]
            outs[f][0, y] = v
            acc = pack_z(acc, v, y, lane)
            if y == 0:
                yl[f * NX + x] = v
            if y == NY - 1:
                yh[f * NX + x] = v
        put_z_face(zf, f * 4 + x // 4, acc, off, lane)

    cond = c_ref[0]
    yl[2 * NX, pl.ds(x, 1), :] = cond[0:1]
    yh[2 * NX, pl.ds(x, 1), :] = cond[NY - 1 : NY]
    zf[8] = jnp.where((lane == 2 * x) | (lane == 2 * x + 1), lane_roll(cond, 2 * x + 1), zf[8])

    @pl.when(x == 0)
    def _():
        for f in range(2):
            for y in range(NY):
                xl[f * NY + y] = outs[f][0, y]
        xl[2 * NY] = cond

    @pl.when(x == NX - 1)
    def _():
        for f in range(2):
            for y in range(NY):
                xh[f * NY + y] = outs[f][0, y]
        xh[2 * NY] = cond


def enter(direction, residual, conductance):
    block = pl.BlockSpec((S, 1, NY, NZ), lambda x: (0, x, 0, 0))
    whole = lambda n: pl.BlockSpec((n, S, NZ), lambda x: (0, 0, 0))
    shape = lambda n: jax.ShapeDtypeStruct((n, S, NZ), F32)
    rows = (33, 33, 33, 33, 9)
    return pl.pallas_call(
        enter_kernel,
        grid=(NX,),
        in_specs=[block, block, pl.BlockSpec((1, NY, NZ), lambda x: (x, 0, 0))],
        out_specs=[pl.BlockSpec((1, NY, S, NZ), lambda x: (x, 0, 0, 0))] * 2 + [whole(n) for n in rows],
        out_shape=[jax.ShapeDtypeStruct((NX, NY, S, NZ), F32)] * 2 + [shape(n) for n in rows],
        compiler_params=grant(4),
        name="enter",
    )(direction, residual, conductance)


def coef_kernel(kappa, cond, xl, xh, yl, yh, zl, zh, out):
    flag = []
    for axis in AXES:
        i, n = lax.axis_index(axis), lax.axis_size(axis)
        flag += [jnp.where(i > 0, 1.0, 0.0).astype(F32), jnp.where(i < n - 1, 1.0, 0.0).astype(F32)]
    lane = lanes((NY, NZ))
    sub = lax.broadcasted_iota(jnp.int32, (NY, NZ), 0)

    def per_x(x, _):
        c = cond[x]
        prev = jnp.where(x == 0, xl[2 * NY] * flag[0], cond[jnp.maximum(x - 1, 0)])
        nxt = jnp.where(x == NX - 1, xh[2 * NY] * flag[1], cond[jnp.minimum(x + 1, NX - 1)])
        ylo = yl[2 * NX, pl.ds(x, 1), :] * flag[2]
        yhi = yh[2 * NX, pl.ds(x, 1), :] * flag[3]
        ym = jnp.where(sub == 0, ylo, pltpu.roll(c, 1, 0))
        yp = jnp.where(sub == NY - 1, yhi, pltpu.roll(c, NY - 1, 0))
        zlo = lane_roll(zl[8], lax.rem(NZ - 2 * x, NZ)) * flag[4]
        zhi = lane_roll(zh[8], NZ - 2 - 2 * x) * flag[5]
        zm = jnp.where(lane == 0, zlo, lane_roll(c, 1))
        zp = jnp.where(lane == NZ - 1, zhi, lane_roll(c, NZ - 1))
        g = [0.5 * (c + n) for n in (prev, nxt, ym, yp, zm, zp)]
        out[0, x] = kappa[x] + ((g[0] + g[1]) + (g[2] + g[3]) + (g[4] + g[5]))
        out[1, x] = jnp.where(x == 0, g[0] * flag[0], g[0])
        out[2, x] = jnp.where(x == NX - 1, g[1] * flag[1], g[1])
        out[3, x] = jnp.where(sub == 0, g[2] * flag[2], g[2])
        out[4, x] = jnp.where(sub == NY - 1, g[3] * flag[3], g[3])
        out[5, x] = jnp.where(lane == 0, g[4] * flag[4], g[4])
        out[6, x] = jnp.where(lane == NZ - 1, g[5] * flag[5], g[5])
        return 0

    lax.fori_loop(0, NX, per_x, 0)


def coefs(kappa, cond, halos):
    return pl.pallas_call(
        coef_kernel,
        in_specs=[VMEM] * 8,
        out_specs=VMEM,
        out_shape=jax.ShapeDtypeStruct((7, NX, NY, NZ), F32),
        compiler_params=grant(4),
        name="coefs",
    )(kappa, cond, *halos)


def stencil_kernel(part, emit, carry, after, field, xl, xh, yl, yh, zl, zh, coef, *refs):
    lane = lanes((S, NZ))
    first, last = lane == 0, lane == NZ - 1
    even = lax.rem(lane, 2) == 0
    others, out, faces = refs[: 5 * carry], refs[5 * carry + after], refs[5 * carry + after + 1 :]
    if emit:
        oxl, oxh, oyl, oyh, ozf = faces

    def per_x(x, edge):
        off = lax.rem(x, 4) * 32
        quarter = x // 4
        beyond = jnp.where(even, lane_roll(zl[part * 4 + quarter], 2), zh[part * 4 + quarter])
        beyond = lane_roll(beyond, lax.rem(NZ - off, NZ))
        acc = jnp.zeros((S, NZ), F32)
        for y in range(NY):
            k = [jnp.broadcast_to(coef[i, x, y : y + 1, :], (S, NZ)) for i in range(7)]
            c = field[x, y]
            xm = xl[part * NY + y] if edge == "lo" else field[x - 1, y]
            xp = xh[part * NY + y] if edge == "hi" else field[x + 1, y]
            ym = field[x, y - 1] if y else yl[part * NX + x]
            yp = field[x, y + 1] if y < NY - 1 else yh[part * NX + x]
            ends = lane_roll(beyond, NZ - 2 - 2 * y)
            zm = jnp.where(first, ends, lane_roll(c, 1))
            zp = jnp.where(last, ends, lane_roll(c, NZ - 1))
            o = ((k[0] * c - k[1] * xm) - (k[2] * xp + k[3] * ym)) - ((k[4] * yp + k[5] * zm) + k[6] * zp)
            out[x, y] = o
            if emit:
                acc = pack_z(acc, o, y, lane)
                if edge == "lo":
                    oxl[y] = o
                if edge == "hi":
                    oxh[y] = o
                if y == 0:
                    oyl[x] = o
                if y == NY - 1:
                    oyh[x] = o
        if emit:
            put_z_face(ozf, quarter, acc, off, lane)

    per_x(jnp.int32(0), "lo")
    lax.fori_loop(1, NX - 1, lambda x, c: (per_x(x, ""), c)[1], 0)
    per_x(jnp.int32(NX - 1), "hi")
    for src, dst in zip(others, faces):
        dst[src.shape[0] :] = src[...]


def stencil(field, halos, coef, part=0, emit=True, carry=(), after=()):
    shape = lambda n: jax.ShapeDtypeStruct((n, S, NZ), F32)
    sent = 2 if carry else 1
    faces = [shape(n * sent) for n in (16, 16, 16, 16, 4)] if emit else []
    out = pl.pallas_call(
        functools.partial(stencil_kernel, part, emit, bool(carry), len(after)),
        in_specs=[VMEM] * (8 + len(carry)) + [pl.BlockSpec(memory_space=pl.ANY)] * len(after),
        out_specs=[VMEM] * (1 + len(faces)),
        out_shape=[jax.ShapeDtypeStruct((NX, NY, S, NZ), F32)] + faces,
        compiler_params=grant(9),
        cost_estimate=pl.CostEstimate(flops=8 << 20, bytes_accessed=12 << 20, transcendentals=0),
        name=f"stencil_{part}_{len(faces)}_{len(carry)}",
    )(field, *halos, coef, *carry, *after)
    return out[0], tuple(out[1:])


def exchange(faces):
    xl, xh, yl, yh, zf = faces
    halos = []
    for axis, low, high in (("gx", xl, xh), ("gy", yl, yh), ("gz", zf, zf)):
        n = lax.axis_size(axis)
        halos.append(lax.ppermute(high, axis, [(j, (j + 1) % n) for j in range(n)]))
        halos.append(lax.ppermute(low, axis, [(j, (j - 1) % n) for j in range(n)]))
    return halos


def split(fields, halves):
    n = 16 * len(fields)
    for y in range(NY):
        for i, ref in enumerate(fields):
            v = ref[0, y]
            hi = v.astype(BF16)
            halves[y, 16 * i : 16 * i + 16, :] = hi
            halves[y, n + 16 * i : n + 16 * i + 16, :] = (v - hi.astype(F32)).astype(BF16)
    return jnp.concatenate([halves[y] for y in range(NY)], axis=1)


def add_up(acc, part):
    x = pl.program_id(0)

    @pl.when(x == 0)
    def _():
        acc[...] = part

    @pl.when(x > 0)
    def _():
        acc[...] = acc[...] + part


def nt(a, b):
    return lax.dot_general(a, b, (((1,), (1,)), ((), ())), preferred_element_type=F32)


def gram_first_kernel(d, q, r, halves, acc):
    op = split((d, q, r), halves)
    add_up(acc, nt(op, op))


def gram_second_kernel(w, z, before, first, halves, gram, acc):
    op = split((w, z), halves)
    every = jnp.concatenate([jnp.concatenate([before[y] for y in range(NY)], axis=1), op], axis=0)
    add_up(acc, nt(every, op))

    @pl.when(pl.program_id(0) == NX - 1)
    def _():
        pad = lambda m: jnp.concatenate([m, jnp.zeros((m.shape[0], 128 - m.shape[1]), F32)], axis=1)
        lane, lane2 = lanes((48, 128)), lanes((32, 128))
        a = pad(first[...])
        a = a[:48] + a[48:]
        a = jnp.where(lane < 48, a + lane_roll(a, 80), 0.0)
        b = pad(acc[...])
        top, low = b[:48] + b[48:96], b[96:128] + b[128:160]
        top = jnp.where(lane < 32, top + lane_roll(top, 96), 0.0)
        low = jnp.where(lane2 < 32, low + lane_roll(low, 96), 0.0)
        a = a + lane_roll(top, 48)
        gram[:32, :] = a[:32] + lane_roll(low, 80)
        gram[32:, :] = a[32:]


FIELD = pl.BlockSpec((1, NY, S, NZ), lambda x: (x, 0, 0, 0))


def gram_first(d, q, r):
    return pl.pallas_call(
        gram_first_kernel,
        grid=(NX,),
        in_specs=[FIELD] * 3,
        out_specs=[pl.BlockSpec((NY, 96, NZ), lambda x: (x, 0, 0)), pl.BlockSpec((96, 96), lambda x: (0, 0))],
        out_shape=[jax.ShapeDtypeStruct((NX * NY, 96, NZ), BF16), jax.ShapeDtypeStruct((96, 96), F32)],
        compiler_params=grant(5),
        cost_estimate=pl.CostEstimate(flops=8 << 20, bytes_accessed=12 << 20, transcendentals=0),
        name="gram_first",
    )(d, q, r)


def gram_second(w, z, halves, first):
    return pl.pallas_call(
        gram_second_kernel,
        grid=(NX,),
        in_specs=[FIELD] * 2
        + [pl.BlockSpec((NY, 96, NZ), lambda x: (x, 0, 0)), pl.BlockSpec((96, 96), lambda x: (0, 0))],
        out_specs=[pl.BlockSpec((NY, 64, NZ), lambda x: (x, 0, 0)), pl.BlockSpec((48, 128), lambda x: (0, 0))],
        out_shape=[jax.ShapeDtypeStruct((NX * NY, 64, NZ), BF16), jax.ShapeDtypeStruct((48, 128), F32)],
        scratch_shapes=[pltpu.VMEM((160, 64), F32)],
        compiler_params=grant(5),
        name="gram_second",
    )(w, z, halves, first)


def add_kernel(*refs):
    total = refs[0][...]
    for ref in refs[1:-1]:
        total = total + ref[...]
    refs[-1][...] = total


def add(*parts):
    return pl.pallas_call(
        add_kernel,
        in_specs=[VMEM] * len(parts),
        out_specs=VMEM,
        out_shape=jax.ShapeDtypeStruct(parts[0].shape, F32),
        compiler_params=grant(1),
        name="add",
    )(*parts)


def gather_parts(part):
    for axis, steps in (("gx", (1, 2, 3)), ("gz", (1, 2, 3)), ("gy", (2, 4, 6))):
        n = lax.axis_size(axis)
        part = add(part, *[lax.ppermute(part, axis, [(j, j ^ s) for j in range(n)]) for s in steps if s < n])
    return part, lax.ppermute(part, "gy", [(j, j ^ 1) for j in range(lax.axis_size("gy"))])


def rows128(m):
    return jnp.concatenate([m, jnp.zeros((128 - m.shape[0], 128), F32)], axis=0)


def mm(a, b):
    return jnp.dot(a, rows128(b), precision=lax.Precision.HIGHEST, preferred_element_type=F32)


def mm_nt(a, b):
    return lax.dot_general(
        a, rows128(b), (((1,), (1,)), ((), ())), precision=lax.Precision.HIGHEST, preferred_element_type=F32
    )


def eye_at(lane, sub, off):
    return jnp.where(lane == sub + off, 1.0, 0.0).astype(F32)


def spd_inverse(m, lane, sub):
    m = jnp.where(lane < 16, m, eye_at(lane, sub, 16))
    for k in range(S):
        row = m[k : k + 1, :]
        row = row / row[:, k : k + 1]
        m = jnp.where(sub == k, row, m - m[:, k : k + 1] * row)
    return jnp.where(lane < 16, lane_roll(m, 112), 0.0)


def factor_inverse(m, lane, sub):
    m = jnp.where(lane < 16, m, eye_at(lane, sub, 16))
    for k in range(S):
        row = m[k : k + 1, :]
        scale = lax.rsqrt(row[:, k : k + 1])
        row = row * scale
        m = jnp.where(sub == k, row, jnp.where(sub > k, m - (m[:, k : k + 1] * scale) * row, m))
    return jnp.where(lane < 16, lane_roll(m, 112), 0.0)


def step(g, lane, sub):
    gd, gq, gr = g[:16], g[16:32], g[32:48]
    low = lane < 16
    curvature = 0.5 * (lane_roll(gd, 112) + gq)
    inv = spd_inverse(curvature, lane, sub)
    s_t = mm(jnp.where(low, gr, 0.0), inv)
    qq = jnp.where(low, lane_roll(gq, 112), 0.0)
    rq = jnp.where(low, lane_roll(gr, 112), 0.0) - mm(s_t, qq)
    c_t = -mm(rq, inv)
    r_t = eye_at(lane, sub, 32) - lane_roll(s_t, 16)
    f_t = r_t + c_t
    ff = mm_nt(mm(f_t, g), f_t)
    ff = 0.5 * (ff + mm_nt(f_t, mm(f_t, g)))
    inv_factor = factor_inverse(ff, lane, sub)
    return s_t, r_t, mm(inv_factor, f_t)


def algebra_kernel(one, two, coef_ref):
    lane = lanes((S, 128))
    sub = lax.broadcasted_iota(jnp.int32, (S, 128), 0)
    lane48, lane32 = lanes((48, 128)), lanes((32, 128))
    g = (one[...] + two[...]) * (1.0 / (64 * 128 * 512))
    g1 = jnp.where(lane48 < 48, g, 0.0)
    s_t, r_t, d_t = step(g1, lane, sub)
    q_t = (
        lane_roll(jnp.where(lane < 16, d_t, 0.0), 16)
        + lane_roll(jnp.where((lane >= 32) & (lane < 48), d_t, 0.0), 16)
        + lane_roll(jnp.where((lane >= 16) & (lane < 32), d_t, 0.0), 48)
    )
    t = jnp.concatenate([d_t, q_t, r_t], axis=0)
    half = jnp.where(lane48 < 48, 0.5 * g, jnp.where(lane48 < 80, g, 0.0))
    corner = lane_roll(0.5 * g[:32], 96)
    corner = jnp.where((lane32 >= 48) & (lane32 < 80), corner, 0.0)
    h = mm(t, jnp.concatenate([half, corner], axis=0))
    g2 = mm_nt(h, t) + mm_nt(t, h)
    s2_t, r2_t, d2_t = step(g2, lane, sub)
    final = mm(jnp.concatenate([s2_t, r2_t, d2_t], axis=0), t)
    final = jnp.concatenate([final[:16] + s_t, final[16:]], axis=0)
    hi = final.astype(BF16).astype(F32)
    for i, part in enumerate((hi, final - hi)):
        coef_ref[48 * i : 48 * i + 48, :128] = jnp.where(lane48 < 48, part, lane_roll(part, 48)).astype(BF16)
        coef_ref[48 * i : 48 * i + 48, 128:] = jnp.where(lane48 < 32, lane_roll(part, 80), 0.0).astype(BF16)


def algebra(one, two):
    return pl.pallas_call(
        algebra_kernel,
        in_specs=[VMEM] * 2,
        out_specs=VMEM,
        out_shape=jax.ShapeDtypeStruct((96, 256), BF16),
        compiler_params=grant(2),
        name="algebra",
    )(one, two)


def leave_kernel(coef, first, second, sol, xo, ro, do):
    left = coef[:, :160]
    flat = [ref.reshape(S * NY, NZ) for ref in (xo, ro, do)]
    inp = sol.reshape(S * NY, NZ)
    for y in range(0, NY, 2):
        rows = [jnp.concatenate([h[y], h[y + 1]], axis=1) for h in (first, second)]
        pair = jnp.concatenate(rows, axis=0)
        res = jnp.dot(left, pair, preferred_element_type=F32)
        res = res[:48] + res[48:]
        for j in range(2):
            v = res[:, j * NZ : (j + 1) * NZ]
            rows = pl.ds(y + j, S, stride=NY)
            flat[0][rows, :] = inp[rows, :] + v[:16]
            flat[1][rows, :] = v[16:32]
            flat[2][rows, :] = v[32:48]


def leave(coef, first, second, sol):
    block = pl.BlockSpec((S, 1, NY, NZ), lambda x: (0, x, 0, 0))
    return pl.pallas_call(
        leave_kernel,
        grid=(NX,),
        in_specs=[pl.BlockSpec((96, 256), lambda x: (0, 0))]
        + [pl.BlockSpec((NY, n, NZ), lambda x: (x, 0, 0)) for n in (96, 64)]
        + [block],
        out_specs=[block] * 3,
        out_shape=[jax.ShapeDtypeStruct((S, NX, NY, NZ), F32)] * 3,
        compiler_params=grant(8),
        name="leave",
    )(coef, first, second, sol)


def body(sol, residual, direction, kappa, cond):
    d, r, *faces = enter(direction, residual, cond)
    start = exchange(faces)
    coef = coefs(kappa, cond, start)
    ld, faces = stencil(d, start, coef)
    halos = exchange(faces)
    lr, lr_faces = stencil(r, start, coef, part=1)
    q, faces = stencil(ld, halos, coef, carry=lr_faces)
    both = exchange(faces)
    halves, gram = gram_first(d, q, r)
    lq, faces = stencil(q, both, coef, after=(gram,))
    halos = exchange(faces)
    w, _ = stencil(lr, both, coef, part=1, emit=False)
    z, _ = stencil(lq, halos, coef, emit=False)
    more, gram = gram_second(w, z, halves, gram)
    return tuple(leave(algebra(*gather_parts(gram)), halves, more, sol))


def solution(mesh):
    fields = P(None, *AXES)
    cells = P(*AXES)
    return jax.shard_map(
        body,
        mesh=mesh,
        in_specs=(fields, fields, fields, cells, cells),
        out_specs=(fields, fields, fields),
        check_vma=False,
    )
```

```python
import functools

import jax
import jax.numpy as jnp
from jax import lax
from jax.experimental import pallas as pl
from jax.experimental.pallas import tpu as pltpu
from jax.sharding import PartitionSpec as P

AXES = ("gx", "gy", "gz")
S = 16
NX, NY, NZ = 16, 16, 128
F32, BF16 = jnp.float32, jnp.bfloat16
VMEM = pl.BlockSpec(memory_space=pltpu.VMEM)


def grant(mib):
    return pltpu.CompilerParams(vmem_limit_bytes=mib << 20)


def lanes(shape):
    return lax.broadcasted_iota(jnp.int32, shape, len(shape) - 1)


def lane_roll(v, shift):
    return pltpu.roll(v, shift, v.ndim - 1)


def pack_z(acc, v, y, lane):
    return jnp.where((lane == 2 * y) | (lane == 2 * y + 1), lane_roll(v, 2 * y + 1), acc)


def put_z_faces(ref, base, staged, lane):
    for q in range(4):
        row = staged[4 * q]
        for j in range(1, 4):
            row = jnp.where(lane >= 32 * j, lane_roll(staged[4 * q + j], 32 * j), row)
        ref[base + q] = row


CHUNK = 4
CHUNKS = NX // CHUNK


def enter_kernel(d_ref, r_ref, c_ref, d_out, r_out, xl, xh, yl, yh, zf, d_in, r_in, c_in, staged, sems):
    lane = lanes((S, NZ))
    pairs = ((d_ref, d_in, d_out), (r_ref, r_in, r_out))
    cond_copy = pltpu.make_async_copy(c_ref, c_in, sems.at[2, 0])
    copies = [
        [
            pltpu.make_async_copy(src.at[:, pl.ds(CHUNK * i, CHUNK)], dst.at[:, pl.ds(CHUNK * i, CHUNK)], sems.at[f, i])
            for f, (src, dst, _) in enumerate(pairs)
        ]
        for i in range(CHUNKS)
    ]
    for group in copies:
        for copy in group:
            copy.start()
    cond_copy.start()

    def per_x(x):
        for f, (_, buf, out) in enumerate(pairs):
            flat = buf.reshape(S * NX * NY, NZ)
            acc = jnp.zeros((S, NZ), F32)
            for y in range(NY):
                v = flat[pl.ds(x * NY + y, S, stride=NX * NY), :]
                out[x, y] = v
                acc = pack_z(acc, v, y, lane)
                if y == 0:
                    yl[f * NX + x] = v
                if y == NY - 1:
                    yh[f * NX + x] = v
            staged[f, x] = acc

    for i, group in enumerate(copies):
        for copy in group:
            copy.wait()
        lax.fori_loop(i * CHUNK // 2, (i + 1) * CHUNK // 2, lambda j, c: (per_x(2 * j), per_x(2 * j + 1), c)[2], 0)
    cond_copy.wait()
    ends = jnp.zeros((S, NZ), F32)
    for x in range(NX):
        cond = c_in[x]
        yl[2 * NX, x : x + 1, :] = cond[0:1]
        yh[2 * NX, x : x + 1, :] = cond[NY - 1 : NY]
        ends = pack_z(ends, cond, x, lane)
    zf[8] = ends
    for f, (_, _, out) in enumerate(pairs):
        put_z_faces(zf, 4 * f, staged.at[f], lane)
        for y in range(NY):
            xl[f * NY + y] = out[0, y]
            xh[f * NY + y] = out[NX - 1, y]
    xl[2 * NY] = c_in[0]
    xh[2 * NY] = c_in[NX - 1]


def enter(direction, residual, conductance):
    shape = lambda n: jax.ShapeDtypeStruct((n, S, NZ), F32)
    rows = (33, 33, 33, 33, 9)
    return pl.pallas_call(
        enter_kernel,
        in_specs=[pl.BlockSpec(memory_space=pltpu.HBM)] * 3,
        out_specs=[VMEM] * 7,
        out_shape=[jax.ShapeDtypeStruct((NX, NY, S, NZ), F32)] * 2 + [shape(n) for n in rows],
        scratch_shapes=[pltpu.VMEM((S, NX, NY, NZ), F32)] * 2
        + [pltpu.VMEM((NX, NY, NZ), F32), pltpu.VMEM((2, NX, S, NZ), F32), pltpu.SemaphoreType.DMA((3, CHUNKS))],
        compiler_params=grant(12),
        name="enter",
    )(*[pltpu.with_memory_space_constraint(v, pltpu.HBM) for v in (direction, residual, conductance)])


def coef_kernel(kappa, cond, xl, xh, yl, yh, zl, zh, out):
    flag = []
    for axis in AXES:
        i, n = lax.axis_index(axis), lax.axis_size(axis)
        flag += [jnp.where(i > 0, 1.0, 0.0).astype(F32), jnp.where(i < n - 1, 1.0, 0.0).astype(F32)]
    lane = lanes((NY, NZ))
    sub = lax.broadcasted_iota(jnp.int32, (NY, NZ), 0)

    def per_x(x, _):
        c = cond[x]
        prev = jnp.where(x == 0, xl[2 * NY] * flag[0], cond[jnp.maximum(x - 1, 0)])
        nxt = jnp.where(x == NX - 1, xh[2 * NY] * flag[1], cond[jnp.minimum(x + 1, NX - 1)])
        ylo = yl[2 * NX, pl.ds(x, 1), :] * flag[2]
        yhi = yh[2 * NX, pl.ds(x, 1), :] * flag[3]
        ym = jnp.where(sub == 0, ylo, pltpu.roll(c, 1, 0))
        yp = jnp.where(sub == NY - 1, yhi, pltpu.roll(c, NY - 1, 0))
        zlo = lane_roll(zl[8], lax.rem(NZ - 2 * x, NZ)) * flag[4]
        zhi = lane_roll(zh[8], NZ - 2 - 2 * x) * flag[5]
        zm = jnp.where(lane == 0, zlo, lane_roll(c, 1))
        zp = jnp.where(lane == NZ - 1, zhi, lane_roll(c, NZ - 1))
        g = [0.5 * (c + n) for n in (prev, nxt, ym, yp, zm, zp)]
        out[0, x] = kappa[x] + ((g[0] + g[1]) + (g[2] + g[3]) + (g[4] + g[5]))
        out[1, x] = jnp.where(x == 0, g[0] * flag[0], g[0])
        out[2, x] = jnp.where(x == NX - 1, g[1] * flag[1], g[1])
        out[3, x] = jnp.where(sub == 0, g[2] * flag[2], g[2])
        out[4, x] = jnp.where(sub == NY - 1, g[3] * flag[3], g[3])
        out[5, x] = jnp.where(lane == 0, g[4] * flag[4], g[4])
        out[6, x] = jnp.where(lane == NZ - 1, g[5] * flag[5], g[5])
        return 0

    lax.fori_loop(0, NX, per_x, 0)


def coefs(kappa, cond, halos):
    return pl.pallas_call(
        coef_kernel,
        in_specs=[VMEM] * 8,
        out_specs=VMEM,
        out_shape=jax.ShapeDtypeStruct((7, NX, NY, NZ), F32),
        compiler_params=grant(4),
        name="coefs",
    )(kappa, cond, *halos)


def stencil_kernel(part, emit, carry, after, field, xl, xh, yl, yh, zl, zh, coef, *refs):
    lane = lanes((S, NZ))
    first, last = lane == 0, lane == NZ - 1
    even = lax.rem(lane, 2) == 0
    others, out, faces = refs[: 5 * carry], refs[5 * carry + after], refs[5 * carry + after + 1 :]
    beyond_rows, staged = refs[-2:]
    if emit:
        oxl, oxh, oyl, oyh, ozf = faces[:5]

    for q in range(4):
        row = jnp.where(even, lane_roll(zl[part * 4 + q], 2), zh[part * 4 + q])
        for j in range(4):
            beyond_rows[4 * q + j] = lane_roll(row, NZ - 32 * j) if j else row

    def per_x(x, edge):
        beyond = beyond_rows[x]
        acc = jnp.zeros((S, NZ), F32)
        for y in range(NY):
            k = [jnp.broadcast_to(coef[i, x, y : y + 1, :], (S, NZ)) for i in range(7)]
            c = field[x, y]
            xm = xl[part * NY + y] if edge == "lo" else field[x - 1, y]
            xp = xh[part * NY + y] if edge == "hi" else field[x + 1, y]
            ym = field[x, y - 1] if y else yl[part * NX + x]
            yp = field[x, y + 1] if y < NY - 1 else yh[part * NX + x]
            ends = lane_roll(beyond, NZ - 2 - 2 * y)
            zm = jnp.where(first, ends, lane_roll(c, 1))
            zp = jnp.where(last, ends, lane_roll(c, NZ - 1))
            o = ((k[0] * c - k[1] * xm) - (k[2] * xp + k[3] * ym)) - ((k[4] * yp + k[5] * zm) + k[6] * zp)
            out[x, y] = o
            if emit:
                acc = pack_z(acc, o, y, lane)
                if edge == "lo":
                    oxl[y] = o
                if edge == "hi":
                    oxh[y] = o
                if y == 0:
                    oyl[x] = o
                if y == NY - 1:
                    oyh[x] = o
        if emit:
            staged[x] = acc

    per_x(0, "lo")
    lax.fori_loop(0, NX // 2 - 1, lambda j, c: (per_x(2 * j + 1, ""), per_x(2 * j + 2, ""), c)[2], 0)
    per_x(NX - 1, "hi")
    if emit:
        put_z_faces(ozf, 0, staged, lane)
    for src, dst in zip(others, faces):
        dst[src.shape[0] :] = src[...]


def stencil(field, halos, coef, part=0, emit=True, carry=(), after=()):
    shape = lambda n: jax.ShapeDtypeStruct((n, S, NZ), F32)
    sent = 2 if carry else 1
    faces = [shape(n * sent) for n in (16, 16, 16, 16, 4)] if emit else []
    out = pl.pallas_call(
        functools.partial(stencil_kernel, part, emit, bool(carry), len(after)),
        in_specs=[VMEM] * (8 + len(carry)) + [pl.BlockSpec(memory_space=pl.ANY)] * len(after),
        out_specs=[VMEM] * (1 + len(faces)),
        out_shape=[jax.ShapeDtypeStruct((NX, NY, S, NZ), F32)] + faces,
        scratch_shapes=[pltpu.VMEM((NX, S, NZ), F32)] * 2,
        compiler_params=grant(9),
        cost_estimate=pl.CostEstimate(flops=8 << 20, bytes_accessed=12 << 20, transcendentals=0),
        name=f"stencil_{part}_{len(faces)}_{len(carry)}",
    )(field, *halos, coef, *carry, *after)
    return out[0], tuple(out[1:])


def exchange(faces):
    xl, xh, yl, yh, zf = faces
    halos = []
    for axis, low, high in (("gx", xl, xh), ("gy", yl, yh), ("gz", zf, zf)):
        n = lax.axis_size(axis)
        halos.append(lax.ppermute(high, axis, [(j, (j + 1) % n) for j in range(n)]))
        halos.append(lax.ppermute(low, axis, [(j, (j - 1) % n) for j in range(n)]))
    return halos


def split(fields, halves, x):
    n = 16 * len(fields)
    for y in range(NY):
        row = x * NY + y
        for i, ref in enumerate(fields):
            v = ref[x, y]
            hi = v.astype(BF16)
            halves[row, 16 * i : 16 * i + 16, :] = hi
            halves[row, n + 16 * i : n + 16 * i + 16, :] = (v - hi.astype(F32)).astype(BF16)
    return side(halves, x)


def side(halves, x):
    return jnp.concatenate([halves[x * NY + y] for y in range(NY)], axis=1)


def nt(a, b):
    return lax.dot_general(a, b, (((1,), (1,)), ((), ())), preferred_element_type=F32)


def gram_first_kernel(d, q, r, halves, acc):
    def per_x(x, c):
        op = split((d, q, r), halves, x)
        acc[...] += nt(op, op)
        return c

    acc[...] = jnp.zeros_like(acc)
    lax.fori_loop(0, NX, per_x, 0)


def gram_second_kernel(w, z, before, first, halves, gram, acc):
    def per_x(x, c):
        op = split((w, z), halves, x)
        acc[...] += nt(jnp.concatenate([side(before, x), op], axis=0), op)
        return c

    acc[...] = jnp.zeros_like(acc)
    lax.fori_loop(0, NX, per_x, 0)
    pad = lambda m: jnp.concatenate([m, jnp.zeros((m.shape[0], 128 - m.shape[1]), F32)], axis=1)
    lane, lane2 = lanes((48, 128)), lanes((32, 128))
    a = pad(first[...])
    a = a[:48] + a[48:]
    a = jnp.where(lane < 48, a + lane_roll(a, 80), 0.0)
    b = pad(acc[...])
    top, low = b[:48] + b[48:96], b[96:128] + b[128:160]
    top = jnp.where(lane < 32, top + lane_roll(top, 96), 0.0)
    low = jnp.where(lane2 < 32, low + lane_roll(low, 96), 0.0)
    a = a + lane_roll(top, 48)
    gram[:32, :] = a[:32] + lane_roll(low, 80)
    gram[32:, :] = a[32:]


def gram_first(d, q, r):
    return pl.pallas_call(
        gram_first_kernel,
        in_specs=[VMEM] * 3,
        out_specs=[VMEM] * 2,
        out_shape=[jax.ShapeDtypeStruct((NX * NY, 96, NZ), BF16), jax.ShapeDtypeStruct((96, 96), F32)],
        compiler_params=grant(14),
        cost_estimate=pl.CostEstimate(flops=8 << 20, bytes_accessed=12 << 20, transcendentals=0),
        name="gram_first",
    )(d, q, r)


def gram_second(w, z, halves, first):
    return pl.pallas_call(
        gram_second_kernel,
        in_specs=[VMEM] * 4,
        out_specs=[VMEM] * 2,
        out_shape=[jax.ShapeDtypeStruct((NX * NY, 64, NZ), BF16), jax.ShapeDtypeStruct((48, 128), F32)],
        scratch_shapes=[pltpu.VMEM((160, 64), F32)],
        compiler_params=grant(18),
        name="gram_second",
    )(w, z, halves, first)


def add_kernel(*refs):
    total = refs[0][...]
    for ref in refs[1:-1]:
        total = total + ref[...]
    refs[-1][...] = total


def add(*parts):
    return pl.pallas_call(
        add_kernel,
        in_specs=[VMEM] * len(parts),
        out_specs=VMEM,
        out_shape=jax.ShapeDtypeStruct(parts[0].shape, F32),
        compiler_params=grant(1),
        name="add",
    )(*parts)


def gather_parts(part):
    for axis, steps in (("gx", (1, 2, 3)), ("gz", (1, 2, 3)), ("gy", (2, 4, 6))):
        n = lax.axis_size(axis)
        part = add(part, *[lax.ppermute(part, axis, [(j, j ^ s) for j in range(n)]) for s in steps if s < n])
    return part, lax.ppermute(part, "gy", [(j, j ^ 1) for j in range(lax.axis_size("gy"))])


def rows128(m):
    return jnp.concatenate([m, jnp.zeros((128 - m.shape[0], 128), F32)], axis=0)


def mm(a, b):
    return jnp.dot(a, rows128(b), precision=lax.Precision.HIGHEST, preferred_element_type=F32)


def mm_nt(a, b):
    return lax.dot_general(
        a, rows128(b), (((1,), (1,)), ((), ())), precision=lax.Precision.HIGHEST, preferred_element_type=F32
    )


def eye_at(lane, sub, off):
    return jnp.where(lane == sub + off, 1.0, 0.0).astype(F32)


def spd_inverse(m, lane, sub):
    m = jnp.where(lane < 16, m, eye_at(lane, sub, 16))
    for k in range(S):
        row = m[k : k + 1, :]
        row = row / row[:, k : k + 1]
        m = jnp.where(sub == k, row, m - m[:, k : k + 1] * row)
    return jnp.where(lane < 16, lane_roll(m, 112), 0.0)


def factor_inverse(m, lane, sub):
    m = jnp.where(lane < 16, m, eye_at(lane, sub, 16))
    for k in range(S):
        row = m[k : k + 1, :]
        scale = lax.rsqrt(row[:, k : k + 1])
        row = row * scale
        m = jnp.where(sub == k, row, jnp.where(sub > k, m - (m[:, k : k + 1] * scale) * row, m))
    return jnp.where(lane < 16, lane_roll(m, 112), 0.0)


def step(g, lane, sub):
    gd, gq, gr = g[:16], g[16:32], g[32:48]
    low = lane < 16
    curvature = 0.5 * (lane_roll(gd, 112) + gq)
    inv = spd_inverse(curvature, lane, sub)
    s_t = mm(jnp.where(low, gr, 0.0), inv)
    qq = jnp.where(low, lane_roll(gq, 112), 0.0)
    rq = jnp.where(low, lane_roll(gr, 112), 0.0) - mm(s_t, qq)
    c_t = -mm(rq, inv)
    r_t = eye_at(lane, sub, 32) - lane_roll(s_t, 16)
    f_t = r_t + c_t
    ff = mm_nt(mm(f_t, g), f_t)
    ff = 0.5 * (ff + mm_nt(f_t, mm(f_t, g)))
    inv_factor = factor_inverse(ff, lane, sub)
    return s_t, r_t, mm(inv_factor, f_t)


def algebra_kernel(one, two, coef_ref):
    lane = lanes((S, 128))
    sub = lax.broadcasted_iota(jnp.int32, (S, 128), 0)
    lane48, lane32 = lanes((48, 128)), lanes((32, 128))
    g = (one[...] + two[...]) * (1.0 / (64 * 128 * 512))
    g1 = jnp.where(lane48 < 48, g, 0.0)
    s_t, r_t, d_t = step(g1, lane, sub)
    q_t = (
        lane_roll(jnp.where(lane < 16, d_t, 0.0), 16)
        + lane_roll(jnp.where((lane >= 32) & (lane < 48), d_t, 0.0), 16)
        + lane_roll(jnp.where((lane >= 16) & (lane < 32), d_t, 0.0), 48)
    )
    t = jnp.concatenate([d_t, q_t, r_t], axis=0)
    half = jnp.where(lane48 < 48, 0.5 * g, jnp.where(lane48 < 80, g, 0.0))
    corner = lane_roll(0.5 * g[:32], 96)
    corner = jnp.where((lane32 >= 48) & (lane32 < 80), corner, 0.0)
    h = mm(t, jnp.concatenate([half, corner], axis=0))
    g2 = mm_nt(h, t) + mm_nt(t, h)
    s2_t, r2_t, d2_t = step(g2, lane, sub)
    final = mm(jnp.concatenate([s2_t, r2_t, d2_t], axis=0), t)
    final = jnp.concatenate([final[:16] + s_t, final[16:]], axis=0)
    hi = final.astype(BF16).astype(F32)
    for i, part in enumerate((hi, final - hi)):
        coef_ref[48 * i : 48 * i + 48, :128] = jnp.where(lane48 < 48, part, lane_roll(part, 48)).astype(BF16)
        coef_ref[48 * i : 48 * i + 48, 128:] = jnp.where(lane48 < 32, lane_roll(part, 80), 0.0).astype(BF16)


def algebra(one, two):
    return pl.pallas_call(
        algebra_kernel,
        in_specs=[VMEM] * 2,
        out_specs=VMEM,
        out_shape=jax.ShapeDtypeStruct((96, 256), BF16),
        compiler_params=grant(2),
        name="algebra",
    )(one, two)


def leave_kernel(coef, first, second, sol, xo, ro, do, x_buf, r_buf, d_buf, sems):
    left = coef[:, :160]
    outs = ((xo, x_buf), (ro, r_buf), (do, d_buf))
    flat = [buf.reshape(S * NX * NY, NZ) for _, buf in outs]
    inp = sol.reshape(S * NX * NY, NZ)

    def per_x(x):
        for y in range(0, NY, 2):
            row = x * NY + y
            pair = [jnp.concatenate([h[row], h[row + 1]], axis=1) for h in (first, second)]
            res = jnp.dot(left, jnp.concatenate(pair, axis=0), preferred_element_type=F32)
            res = res[:48] + res[48:]
            for j in range(2):
                v = res[:, j * NZ : (j + 1) * NZ]
                rows = pl.ds(row + j, S, stride=NX * NY)
                flat[0][rows, :] = inp[rows, :] + v[:16]
                flat[1][rows, :] = v[16:32]
                flat[2][rows, :] = v[32:48]

    copies = []
    for i in range(CHUNKS):
        lax.fori_loop(i * CHUNK // 2, (i + 1) * CHUNK // 2, lambda j, c: (per_x(2 * j), per_x(2 * j + 1), c)[2], 0)
        part = pl.ds(CHUNK * i, CHUNK)
        for k, (out, buf) in enumerate(outs):
            copies.append(pltpu.make_async_copy(buf.at[:, part], out.at[:, part], sems.at[k, i]))
            copies[-1].start()
    for copy in copies:
        copy.wait()


def leave(coef, first, second, sol):
    return pl.pallas_call(
        leave_kernel,
        in_specs=[VMEM] * 4,
        out_specs=[pl.BlockSpec(memory_space=pltpu.HBM)] * 3,
        out_shape=[jax.ShapeDtypeStruct((S, NX, NY, NZ), F32)] * 3,
        scratch_shapes=[pltpu.VMEM((S, NX, NY, NZ), F32)] * 3 + [pltpu.SemaphoreType.DMA((3, CHUNKS))],
        compiler_params=grant(24),
        name="leave",
    )(coef, first, second, sol)


def body(sol, residual, direction, kappa, cond):
    d, r, *faces = enter(direction, residual, cond)
    start = exchange(faces)
    coef = coefs(kappa, cond, start)
    ld, faces = stencil(d, start, coef)
    halos = exchange(faces)
    lr, lr_faces = stencil(r, start, coef, part=1)
    q, faces = stencil(ld, halos, coef, carry=lr_faces)
    both = exchange(faces)
    halves, gram = gram_first(d, q, r)
    lq, faces = stencil(q, both, coef, after=(gram,))
    halos = exchange(faces)
    w, _ = stencil(lr, both, coef, part=1, emit=False)
    z, _ = stencil(lq, halos, coef, emit=False)
    more, gram = gram_second(w, z, halves, gram)
    return tuple(leave(algebra(*gather_parts(gram)), halves, more, sol))


def solution(mesh):
    fields = P(None, *AXES)
    cells = P(*AXES)
    return jax.shard_map(
        body,
        mesh=mesh,
        in_specs=(fields, fields, fields, cells, cells),
        out_specs=(fields, fields, fields),
        check_vma=False,
    )
```

```python
import functools

import jax
import jax.numpy as jnp
from jax import lax
from jax.experimental import pallas as pl
from jax.experimental.pallas import tpu as pltpu
from jax.sharding import PartitionSpec as P

AXES = ("gx", "gy", "gz")
S = 16
NX, NY, NZ = 16, 16, 128
F32, BF16 = jnp.float32, jnp.bfloat16
VMEM = pl.BlockSpec(memory_space=pltpu.VMEM)


def grant(mib):
    return pltpu.CompilerParams(vmem_limit_bytes=mib << 20)


def lanes(shape):
    return lax.broadcasted_iota(jnp.int32, shape, len(shape) - 1)


def lane_roll(v, shift):
    return pltpu.roll(v, shift, v.ndim - 1)


def pack_z(acc, v, y, lane):
    return acc + lane_roll(jnp.where((lane == 0) | (lane == NZ - 1), v, 0.0), 2 * y + 1)


def put_z_faces(ref, base, staged, lane):
    for q in range(4):
        row = staged[4 * q]
        for j in range(1, 4):
            row = jnp.where(lane >= 32 * j, lane_roll(staged[4 * q + j], 32 * j), row)
        ref[base + q] = row


CHUNK = 4
CHUNKS = NX // CHUNK


def enter_kernel(d_ref, r_ref, c_ref, d_out, r_out, xl, xh, yl, yh, zf, d_in, r_in, c_in, staged, sems):
    lane = lanes((S, NZ))
    pairs = ((d_ref, d_in, d_out), (r_ref, r_in, r_out))
    cond_copy = pltpu.make_async_copy(c_ref, c_in, sems.at[2, 0])
    copies = [
        [
            pltpu.make_async_copy(src.at[:, pl.ds(CHUNK * i, CHUNK)], dst.at[:, pl.ds(CHUNK * i, CHUNK)], sems.at[f, i])
            for f, (src, dst, _) in enumerate(pairs)
        ]
        for i in range(CHUNKS)
    ]
    for group in copies:
        for copy in group:
            copy.start()
    cond_copy.start()

    def per_x(x):
        for f, (_, buf, out) in enumerate(pairs):
            flat = buf.reshape(S * NX * NY, NZ)
            acc = jnp.zeros((S, NZ), F32)
            for y in range(NY):
                v = flat[pl.ds(x * NY + y, S, stride=NX * NY), :]
                out[x, y] = v
                acc = pack_z(acc, v, y, lane)
                if y == 0:
                    yl[f * NX + x] = v
                if y == NY - 1:
                    yh[f * NX + x] = v
            staged[f, x] = acc

    for i, group in enumerate(copies):
        for copy in group:
            copy.wait()
        lax.fori_loop(i * CHUNK // 2, (i + 1) * CHUNK // 2, lambda j, c: (per_x(2 * j), per_x(2 * j + 1), c)[2], 0)
    cond_copy.wait()
    ends = jnp.zeros((S, NZ), F32)
    for x in range(NX):
        cond = c_in[x]
        yl[2 * NX, x : x + 1, :] = cond[0:1]
        yh[2 * NX, x : x + 1, :] = cond[NY - 1 : NY]
        ends = pack_z(ends, cond, x, lane)
    zf[8] = ends
    for f, (_, _, out) in enumerate(pairs):
        put_z_faces(zf, 4 * f, staged.at[f], lane)
        for y in range(NY):
            xl[f * NY + y] = out[0, y]
            xh[f * NY + y] = out[NX - 1, y]
    xl[2 * NY] = c_in[0]
    xh[2 * NY] = c_in[NX - 1]


def enter(direction, residual, conductance):
    shape = lambda n: jax.ShapeDtypeStruct((n, S, NZ), F32)
    rows = (33, 33, 33, 33, 9)
    return pl.pallas_call(
        enter_kernel,
        in_specs=[pl.BlockSpec(memory_space=pltpu.HBM)] * 3,
        out_specs=[VMEM] * 7,
        out_shape=[jax.ShapeDtypeStruct((NX, NY, S, NZ), F32)] * 2 + [shape(n) for n in rows],
        scratch_shapes=[pltpu.VMEM((S, NX, NY, NZ), F32)] * 2
        + [pltpu.VMEM((NX, NY, NZ), F32), pltpu.VMEM((2, NX, S, NZ), F32), pltpu.SemaphoreType.DMA((3, CHUNKS))],
        compiler_params=grant(12),
        name="enter",
    )(*[pltpu.with_memory_space_constraint(v, pltpu.HBM) for v in (direction, residual, conductance)])


def coef_kernel(kappa, cond, xl, xh, yl, yh, zl, zh, out):
    flag = []
    for axis in AXES:
        i, n = lax.axis_index(axis), lax.axis_size(axis)
        flag += [jnp.where(i > 0, 1.0, 0.0).astype(F32), jnp.where(i < n - 1, 1.0, 0.0).astype(F32)]
    lane = lanes((NY, NZ))
    sub = lax.broadcasted_iota(jnp.int32, (NY, NZ), 0)

    def per_x(x, _):
        c = cond[x]
        prev = jnp.where(x == 0, xl[2 * NY] * flag[0], cond[jnp.maximum(x - 1, 0)])
        nxt = jnp.where(x == NX - 1, xh[2 * NY] * flag[1], cond[jnp.minimum(x + 1, NX - 1)])
        ylo = yl[2 * NX, pl.ds(x, 1), :] * flag[2]
        yhi = yh[2 * NX, pl.ds(x, 1), :] * flag[3]
        ym = jnp.where(sub == 0, ylo, pltpu.roll(c, 1, 0))
        yp = jnp.where(sub == NY - 1, yhi, pltpu.roll(c, NY - 1, 0))
        zlo = lane_roll(zl[8], lax.rem(NZ - 2 * x, NZ)) * flag[4]
        zhi = lane_roll(zh[8], NZ - 2 - 2 * x) * flag[5]
        zm = jnp.where(lane == 0, zlo, lane_roll(c, 1))
        zp = jnp.where(lane == NZ - 1, zhi, lane_roll(c, NZ - 1))
        g = [0.5 * (c + n) for n in (prev, nxt, ym, yp, zm, zp)]
        out[0, x] = kappa[x] + ((g[0] + g[1]) + (g[2] + g[3]) + (g[4] + g[5]))
        out[1, x] = jnp.where(x == 0, g[0] * flag[0], g[0])
        out[2, x] = jnp.where(x == NX - 1, g[1] * flag[1], g[1])
        out[3, x] = jnp.where(sub == 0, g[2] * flag[2], g[2])
        out[4, x] = jnp.where(sub == NY - 1, g[3] * flag[3], g[3])
        out[5, x] = jnp.where(lane == 0, g[4] * flag[4], g[4])
        out[6, x] = jnp.where(lane == NZ - 1, g[5] * flag[5], g[5])
        return 0

    lax.fori_loop(0, NX, per_x, 0)


def coefs(kappa, cond, halos):
    return pl.pallas_call(
        coef_kernel,
        in_specs=[VMEM] * 8,
        out_specs=VMEM,
        out_shape=jax.ShapeDtypeStruct((7, NX, NY, NZ), F32),
        compiler_params=grant(4),
        name="coefs",
    )(kappa, cond, *halos)


def stencil_kernel(part, emit, carry, after, field, xl, xh, yl, yh, zl, zh, coef, *refs):
    lane = lanes((S, NZ))
    first, last = lane == 0, lane == NZ - 1
    even = lax.rem(lane, 2) == 0
    others, out, faces = refs[: 5 * carry], refs[5 * carry + after], refs[5 * carry + after + 1 :]
    beyond_rows, staged = refs[-2:]
    if emit:
        oxl, oxh, oyl, oyh, ozf = faces[:5]

    for q in range(4):
        row = jnp.where(even, lane_roll(zl[part * 4 + q], 2), zh[part * 4 + q])
        for j in range(4):
            beyond_rows[4 * q + j] = lane_roll(row, NZ - 32 * j) if j else row

    def per_x(x, edge):
        beyond = beyond_rows[x]
        for y in range(NY):
            k = [jnp.broadcast_to(coef[i, x, y : y + 1, :], (S, NZ)) for i in range(7)]
            c = field[x, y]
            xm = xl[part * NY + y] if edge == "lo" else field[x - 1, y]
            xp = xh[part * NY + y] if edge == "hi" else field[x + 1, y]
            ym = field[x, y - 1] if y else yl[part * NX + x]
            yp = field[x, y + 1] if y < NY - 1 else yh[part * NX + x]
            ends = lane_roll(beyond, NZ - 2 - 2 * y)
            zm = jnp.where(first, ends, lane_roll(c, 1))
            zp = jnp.where(last, ends, lane_roll(c, NZ - 1))
            o = ((k[0] * c - k[1] * xm) - (k[2] * xp + k[3] * ym)) - ((k[4] * yp + k[5] * zm) + k[6] * zp)
            out[x, y] = o
            if emit:
                if edge == "lo":
                    oxl[y] = o
                if edge == "hi":
                    oxh[y] = o
                if y == 0:
                    oyl[x] = o
                if y == NY - 1:
                    oyh[x] = o

    per_x(0, "lo")
    lax.fori_loop(0, NX // 2 - 1, lambda j, c: (per_x(2 * j + 1, ""), per_x(2 * j + 2, ""), c)[2], 0)
    per_x(NX - 1, "hi")
    if emit:

        def ends_of(x):
            acc = jnp.zeros((S, NZ), F32)
            for y in range(NY):
                acc = pack_z(acc, out[x, y], y, lane)
            staged[x] = acc

        lax.fori_loop(0, NX // 4, lambda j, c: ([ends_of(4 * j + i) for i in range(4)], c)[1], 0)
        put_z_faces(ozf, 0, staged, lane)
    for src, dst in zip(others, faces):
        dst[src.shape[0] :] = src[...]


def stencil(field, halos, coef, part=0, emit=True, carry=(), after=()):
    shape = lambda n: jax.ShapeDtypeStruct((n, S, NZ), F32)
    sent = 2 if carry else 1
    faces = [shape(n * sent) for n in (16, 16, 16, 16, 4)] if emit else []
    out = pl.pallas_call(
        functools.partial(stencil_kernel, part, emit, bool(carry), len(after)),
        in_specs=[VMEM] * (8 + len(carry)) + [pl.BlockSpec(memory_space=pl.ANY)] * len(after),
        out_specs=[VMEM] * (1 + len(faces)),
        out_shape=[jax.ShapeDtypeStruct((NX, NY, S, NZ), F32)] + faces,
        scratch_shapes=[pltpu.VMEM((NX, S, NZ), F32)] * 2,
        compiler_params=grant(9),
        cost_estimate=pl.CostEstimate(flops=8 << 20, bytes_accessed=12 << 20, transcendentals=0),
        name=f"stencil_{part}_{len(faces)}_{len(carry)}",
    )(field, *halos, coef, *carry, *after)
    return out[0], tuple(out[1:])


def exchange(faces):
    xl, xh, yl, yh, zf = faces
    halos = []
    for axis, low, high in (("gx", xl, xh), ("gy", yl, yh), ("gz", zf, zf)):
        n = lax.axis_size(axis)
        halos.append(lax.ppermute(high, axis, [(j, (j + 1) % n) for j in range(n)]))
        halos.append(lax.ppermute(low, axis, [(j, (j - 1) % n) for j in range(n)]))
    return halos


def split(fields, halves, x):
    n = 16 * len(fields)
    for y in range(NY):
        row = x * NY + y
        for i, ref in enumerate(fields):
            v = ref[x, y]
            hi = v.astype(BF16)
            halves[row, 16 * i : 16 * i + 16, :] = hi
            halves[row, n + 16 * i : n + 16 * i + 16, :] = (v - hi.astype(F32)).astype(BF16)
    return side(halves, x)


def side(halves, x):
    return jnp.concatenate([halves[x * NY + y] for y in range(NY)], axis=1)


def nt(a, b):
    return lax.dot_general(a, b, (((1,), (1,)), ((), ())), preferred_element_type=F32)


def gram_first_kernel(d, q, r, halves, acc):
    def per_x(x, c):
        op = split((d, q, r), halves, x)
        acc[...] += nt(op, op)
        return c

    acc[...] = jnp.zeros_like(acc)
    lax.fori_loop(0, NX // 2, lambda j, c: per_x(2 * j + 1, per_x(2 * j, c)), 0)


def gram_second_kernel(w, z, before, first, halves, gram, acc):
    def per_x(x, c):
        op = split((w, z), halves, x)
        acc[...] += nt(jnp.concatenate([side(before, x), op], axis=0), op)
        return c

    acc[...] = jnp.zeros_like(acc)
    lax.fori_loop(0, NX // 2, lambda j, c: per_x(2 * j + 1, per_x(2 * j, c)), 0)
    pad = lambda m: jnp.concatenate([m, jnp.zeros((m.shape[0], 128 - m.shape[1]), F32)], axis=1)
    lane, lane2 = lanes((48, 128)), lanes((32, 128))
    a = pad(first[...])
    a = a[:48] + a[48:]
    a = jnp.where(lane < 48, a + lane_roll(a, 80), 0.0)
    b = pad(acc[...])
    top, low = b[:48] + b[48:96], b[96:128] + b[128:160]
    top = jnp.where(lane < 32, top + lane_roll(top, 96), 0.0)
    low = jnp.where(lane2 < 32, low + lane_roll(low, 96), 0.0)
    a = a + lane_roll(top, 48)
    gram[:32, :] = a[:32] + lane_roll(low, 80)
    gram[32:, :] = a[32:]


def gram_first(d, q, r):
    return pl.pallas_call(
        gram_first_kernel,
        in_specs=[VMEM] * 3,
        out_specs=[VMEM] * 2,
        out_shape=[jax.ShapeDtypeStruct((NX * NY, 96, NZ), BF16), jax.ShapeDtypeStruct((96, 96), F32)],
        compiler_params=grant(14),
        cost_estimate=pl.CostEstimate(flops=8 << 20, bytes_accessed=12 << 20, transcendentals=0),
        name="gram_first",
    )(d, q, r)


def gram_second(w, z, halves, first):
    return pl.pallas_call(
        gram_second_kernel,
        in_specs=[VMEM] * 4,
        out_specs=[VMEM] * 2,
        out_shape=[jax.ShapeDtypeStruct((NX * NY, 64, NZ), BF16), jax.ShapeDtypeStruct((48, 128), F32)],
        scratch_shapes=[pltpu.VMEM((160, 64), F32)],
        compiler_params=grant(18),
        name="gram_second",
    )(w, z, halves, first)


def add_kernel(*refs):
    total = refs[0][...]
    for ref in refs[1:-1]:
        total = total + ref[...]
    refs[-1][...] = total


def add(*parts):
    return pl.pallas_call(
        add_kernel,
        in_specs=[VMEM] * len(parts),
        out_specs=VMEM,
        out_shape=jax.ShapeDtypeStruct(parts[0].shape, F32),
        compiler_params=grant(1),
        name="add",
    )(*parts)


def gather_parts(part):
    for axis, steps in (("gx", (1, 2, 3)), ("gz", (1, 2, 3)), ("gy", (2, 4, 6))):
        n = lax.axis_size(axis)
        part = add(part, *[lax.ppermute(part, axis, [(j, j ^ s) for j in range(n)]) for s in steps if s < n])
    return part, lax.ppermute(part, "gy", [(j, j ^ 1) for j in range(lax.axis_size("gy"))])


def rows128(m):
    return jnp.concatenate([m, jnp.zeros((128 - m.shape[0], 128), F32)], axis=0)


def mm(a, b):
    return jnp.dot(a, rows128(b), precision=lax.Precision.HIGHEST, preferred_element_type=F32)


def mm_nt(a, b):
    return lax.dot_general(
        a, rows128(b), (((1,), (1,)), ((), ())), precision=lax.Precision.HIGHEST, preferred_element_type=F32
    )


def eye_at(lane, sub, off):
    return jnp.where(lane == sub + off, 1.0, 0.0).astype(F32)


def spd_inverse(m, lane, sub):
    m = jnp.where(lane < 16, m, eye_at(lane, sub, 16))
    for k in range(S):
        row = m[k : k + 1, :]
        row = row / row[:, k : k + 1]
        m = jnp.where(sub == k, row, m - m[:, k : k + 1] * row)
    return jnp.where(lane < 16, lane_roll(m, 112), 0.0)


def factor_inverse(m, lane, sub):
    m = jnp.where(lane < 16, m, eye_at(lane, sub, 16))
    for k in range(S):
        row = m[k : k + 1, :]
        scale = lax.rsqrt(row[:, k : k + 1])
        row = row * scale
        m = jnp.where(sub == k, row, jnp.where(sub > k, m - (m[:, k : k + 1] * scale) * row, m))
    return jnp.where(lane < 16, lane_roll(m, 112), 0.0)


def step(g, lane, sub):
    gd, gq, gr = g[:16], g[16:32], g[32:48]
    low = lane < 16
    curvature = 0.5 * (lane_roll(gd, 112) + gq)
    inv = spd_inverse(curvature, lane, sub)
    s_t = mm(jnp.where(low, gr, 0.0), inv)
    qq = jnp.where(low, lane_roll(gq, 112), 0.0)
    rq = jnp.where(low, lane_roll(gr, 112), 0.0) - mm(s_t, qq)
    c_t = -mm(rq, inv)
    r_t = eye_at(lane, sub, 32) - lane_roll(s_t, 16)
    f_t = r_t + c_t
    ff = mm_nt(mm(f_t, g), f_t)
    ff = 0.5 * (ff + mm_nt(f_t, mm(f_t, g)))
    inv_factor = factor_inverse(ff, lane, sub)
    return s_t, r_t, mm(inv_factor, f_t)


def algebra_kernel(one, two, coef_ref):
    lane = lanes((S, 128))
    sub = lax.broadcasted_iota(jnp.int32, (S, 128), 0)
    lane48, lane32 = lanes((48, 128)), lanes((32, 128))
    g = (one[...] + two[...]) * (1.0 / (64 * 128 * 512))
    g1 = jnp.where(lane48 < 48, g, 0.0)
    s_t, r_t, d_t = step(g1, lane, sub)
    q_t = (
        lane_roll(jnp.where(lane < 16, d_t, 0.0), 16)
        + lane_roll(jnp.where((lane >= 32) & (lane < 48), d_t, 0.0), 16)
        + lane_roll(jnp.where((lane >= 16) & (lane < 32), d_t, 0.0), 48)
    )
    t = jnp.concatenate([d_t, q_t, r_t], axis=0)
    half = jnp.where(lane48 < 48, 0.5 * g, jnp.where(lane48 < 80, g, 0.0))
    corner = lane_roll(0.5 * g[:32], 96)
    corner = jnp.where((lane32 >= 48) & (lane32 < 80), corner, 0.0)
    h = mm(t, jnp.concatenate([half, corner], axis=0))
    g2 = mm_nt(h, t) + mm_nt(t, h)
    s2_t, r2_t, d2_t = step(g2, lane, sub)
    final = mm(jnp.concatenate([s2_t, r2_t, d2_t], axis=0), t)
    final = jnp.concatenate([final[:16] + s_t, final[16:]], axis=0)
    hi = final.astype(BF16).astype(F32)
    for i, part in enumerate((hi, final - hi)):
        coef_ref[48 * i : 48 * i + 48, :128] = jnp.where(lane48 < 48, part, lane_roll(part, 48)).astype(BF16)
        coef_ref[48 * i : 48 * i + 48, 128:] = jnp.where(lane48 < 32, lane_roll(part, 80), 0.0).astype(BF16)


def algebra(one, two):
    return pl.pallas_call(
        algebra_kernel,
        in_specs=[VMEM] * 2,
        out_specs=VMEM,
        out_shape=jax.ShapeDtypeStruct((96, 256), BF16),
        compiler_params=grant(2),
        name="algebra",
    )(one, two)


def leave_kernel(coef, first, second, sol, xo, ro, do, x_buf, r_buf, d_buf, sems):
    left = coef[:, :160]
    outs = ((xo, x_buf), (ro, r_buf), (do, d_buf))
    flat = [buf.reshape(S * NX * NY, NZ) for _, buf in outs]
    inp = sol.reshape(S * NX * NY, NZ)

    def per_x(x):
        for y in range(0, NY, 2):
            row = x * NY + y
            pair = [jnp.concatenate([h[row], h[row + 1]], axis=1) for h in (first, second)]
            res = jnp.dot(left, jnp.concatenate(pair, axis=0), preferred_element_type=F32)
            res = res[:48] + res[48:]
            for j in range(2):
                v = res[:, j * NZ : (j + 1) * NZ]
                rows = pl.ds(row + j, S, stride=NX * NY)
                flat[0][rows, :] = inp[rows, :] + v[:16]
                flat[1][rows, :] = v[16:32]
                flat[2][rows, :] = v[32:48]

    copies = []
    for i in range(CHUNKS):
        lax.fori_loop(i * CHUNK // 2, (i + 1) * CHUNK // 2, lambda j, c: (per_x(2 * j), per_x(2 * j + 1), c)[2], 0)
        part = pl.ds(CHUNK * i, CHUNK)
        for k, (out, buf) in enumerate(outs):
            copies.append(pltpu.make_async_copy(buf.at[:, part], out.at[:, part], sems.at[k, i]))
            copies[-1].start()
    for copy in copies:
        copy.wait()


def leave(coef, first, second, sol):
    return pl.pallas_call(
        leave_kernel,
        in_specs=[VMEM] * 4,
        out_specs=[pl.BlockSpec(memory_space=pltpu.HBM)] * 3,
        out_shape=[jax.ShapeDtypeStruct((S, NX, NY, NZ), F32)] * 3,
        scratch_shapes=[pltpu.VMEM((S, NX, NY, NZ), F32)] * 3 + [pltpu.SemaphoreType.DMA((3, CHUNKS))],
        compiler_params=grant(24),
        name="leave",
    )(coef, first, second, sol)


def body(sol, residual, direction, kappa, cond):
    d, r, *faces = enter(direction, residual, cond)
    start = exchange(faces)
    coef = coefs(kappa, cond, start)
    ld, faces = stencil(d, start, coef)
    halos = exchange(faces)
    lr, lr_faces = stencil(r, start, coef, part=1)
    q, faces = stencil(ld, halos, coef, carry=lr_faces)
    both = exchange(faces)
    halves, gram = gram_first(d, q, r)
    lq, faces = stencil(q, both, coef, after=(gram,))
    halos = exchange(faces)
    w, _ = stencil(lr, both, coef, part=1, emit=False)
    z, _ = stencil(lq, halos, coef, emit=False)
    more, gram = gram_second(w, z, halves, gram)
    return tuple(leave(algebra(*gather_parts(gram)), halves, more, sol))


def solution(mesh):
    fields = P(None, *AXES)
    cells = P(*AXES)
    return jax.shard_map(
        body,
        mesh=mesh,
        in_specs=(fields, fields, fields, cells, cells),
        out_specs=(fields, fields, fields),
        check_vma=False,
    )
```

```python
import functools

import jax
import jax.numpy as jnp
from jax import lax
from jax.experimental import pallas as pl
from jax.experimental.pallas import tpu as pltpu
from jax.sharding import PartitionSpec as P

AXES = ("gx", "gy", "gz")
S = 16
NX, NY, NZ = 16, 16, 128
F32, BF16 = jnp.float32, jnp.bfloat16
VMEM = pl.BlockSpec(memory_space=pltpu.VMEM)


def grant(mib):
    return pltpu.CompilerParams(vmem_limit_bytes=mib << 20)


def lanes(shape):
    return lax.broadcasted_iota(jnp.int32, shape, len(shape) - 1)


def lane_roll(v, shift):
    return pltpu.roll(v, shift, v.ndim - 1)


def pack_z(acc, v, y, lane):
    return acc + lane_roll(jnp.where((lane == 0) | (lane == NZ - 1), v, 0.0), 2 * y + 1)


def put_z_faces(ref, base, staged, lane):
    for q in range(4):
        row = staged[4 * q]
        for j in range(1, 4):
            row = jnp.where(lane >= 32 * j, lane_roll(staged[4 * q + j], 32 * j), row)
        ref[base + q] = row


CHUNK = 4
CHUNKS = NX // CHUNK


def enter_kernel(d_ref, r_ref, c_ref, d_out, r_out, xl, xh, yl, yh, zf, d_in, r_in, c_in, staged, sems):
    lane = lanes((S, NZ))
    pairs = ((d_ref, d_in, d_out), (r_ref, r_in, r_out))
    cond_copy = pltpu.make_async_copy(c_ref, c_in, sems.at[2, 0])
    copies = [
        [
            pltpu.make_async_copy(src.at[:, pl.ds(CHUNK * i, CHUNK)], dst.at[:, pl.ds(CHUNK * i, CHUNK)], sems.at[f, i])
            for f, (src, dst, _) in enumerate(pairs)
        ]
        for i in range(CHUNKS)
    ]
    for group in copies:
        for copy in group:
            copy.start()
    cond_copy.start()

    def per_x(x):
        for f, (_, buf, out) in enumerate(pairs):
            flat = buf.reshape(S * NX * NY, NZ)
            acc = jnp.zeros((S, NZ), F32)
            for y in range(NY):
                v = flat[pl.ds(x * NY + y, S, stride=NX * NY), :]
                out[x, y] = v
                acc = pack_z(acc, v, y, lane)
                if y == 0:
                    yl[f * NX + x] = v
                if y == NY - 1:
                    yh[f * NX + x] = v
            staged[f, x] = acc

    for i, group in enumerate(copies):
        for copy in group:
            copy.wait()
        lax.fori_loop(i * CHUNK // 2, (i + 1) * CHUNK // 2, lambda j, c: (per_x(2 * j), per_x(2 * j + 1), c)[2], 0)
    cond_copy.wait()
    ends = jnp.zeros((S, NZ), F32)
    for x in range(NX):
        cond = c_in[x]
        yl[2 * NX, x : x + 1, :] = cond[0:1]
        yh[2 * NX, x : x + 1, :] = cond[NY - 1 : NY]
        ends = pack_z(ends, cond, x, lane)
    zf[8] = ends
    for f, (_, _, out) in enumerate(pairs):
        put_z_faces(zf, 4 * f, staged.at[f], lane)
        for y in range(NY):
            xl[f * NY + y] = out[0, y]
            xh[f * NY + y] = out[NX - 1, y]
    xl[2 * NY] = c_in[0]
    xh[2 * NY] = c_in[NX - 1]


def enter(direction, residual, conductance):
    shape = lambda n: jax.ShapeDtypeStruct((n, S, NZ), F32)
    rows = (33, 33, 33, 33, 9)
    return pl.pallas_call(
        enter_kernel,
        in_specs=[pl.BlockSpec(memory_space=pltpu.HBM)] * 3,
        out_specs=[VMEM] * 7,
        out_shape=[jax.ShapeDtypeStruct((NX, NY, S, NZ), F32)] * 2 + [shape(n) for n in rows],
        scratch_shapes=[pltpu.VMEM((S, NX, NY, NZ), F32)] * 2
        + [pltpu.VMEM((NX, NY, NZ), F32), pltpu.VMEM((2, NX, S, NZ), F32), pltpu.SemaphoreType.DMA((3, CHUNKS))],
        compiler_params=grant(12),
        name="enter",
    )(*[pltpu.with_memory_space_constraint(v, pltpu.HBM) for v in (direction, residual, conductance)])


def coef_kernel(kappa, cond, xl, xh, yl, yh, zl, zh, out):
    flag = []
    for axis in AXES:
        i, n = lax.axis_index(axis), lax.axis_size(axis)
        flag += [jnp.where(i > 0, 1.0, 0.0).astype(F32), jnp.where(i < n - 1, 1.0, 0.0).astype(F32)]
    lane = lanes((NY, NZ))
    sub = lax.broadcasted_iota(jnp.int32, (NY, NZ), 0)

    def per_x(x, _):
        c = cond[x]
        prev = jnp.where(x == 0, xl[2 * NY] * flag[0], cond[jnp.maximum(x - 1, 0)])
        nxt = jnp.where(x == NX - 1, xh[2 * NY] * flag[1], cond[jnp.minimum(x + 1, NX - 1)])
        ylo = yl[2 * NX, pl.ds(x, 1), :] * flag[2]
        yhi = yh[2 * NX, pl.ds(x, 1), :] * flag[3]
        ym = jnp.where(sub == 0, ylo, pltpu.roll(c, 1, 0))
        yp = jnp.where(sub == NY - 1, yhi, pltpu.roll(c, NY - 1, 0))
        zlo = lane_roll(zl[8], lax.rem(NZ - 2 * x, NZ)) * flag[4]
        zhi = lane_roll(zh[8], NZ - 2 - 2 * x) * flag[5]
        zm = jnp.where(lane == 0, zlo, lane_roll(c, 1))
        zp = jnp.where(lane == NZ - 1, zhi, lane_roll(c, NZ - 1))
        g = [0.5 * (c + n) for n in (prev, nxt, ym, yp, zm, zp)]
        out[0, x] = kappa[x] + ((g[0] + g[1]) + (g[2] + g[3]) + (g[4] + g[5]))
        out[1, x] = jnp.where(x == 0, g[0] * flag[0], g[0])
        out[2, x] = jnp.where(x == NX - 1, g[1] * flag[1], g[1])
        out[3, x] = jnp.where(sub == 0, g[2] * flag[2], g[2])
        out[4, x] = jnp.where(sub == NY - 1, g[3] * flag[3], g[3])
        out[5, x] = jnp.where(lane == 0, g[4] * flag[4], g[4])
        out[6, x] = jnp.where(lane == NZ - 1, g[5] * flag[5], g[5])
        return 0

    lax.fori_loop(0, NX, per_x, 0)


def coefs(kappa, cond, halos):
    return pl.pallas_call(
        coef_kernel,
        in_specs=[VMEM] * 8,
        out_specs=VMEM,
        out_shape=jax.ShapeDtypeStruct((7, NX, NY, NZ), F32),
        compiler_params=grant(4),
        name="coefs",
    )(kappa, cond, *halos)


def stencil_kernel(part, emit, carry, after, field, xl, xh, yl, yh, zl, zh, coef, *refs):
    lane = lanes((S, NZ))
    first, last = lane == 0, lane == NZ - 1
    even = lax.rem(lane, 2) == 0
    others, out, faces = refs[: 5 * carry], refs[5 * carry + after], refs[5 * carry + after + 1 :]
    beyond_rows, staged = refs[-2:]
    if emit:
        oxl, oxh, oyl, oyh, ozf = faces[:5]

    for q in range(4):
        row = jnp.where(even, lane_roll(zl[part * 4 + q], 2), zh[part * 4 + q])
        for j in range(4):
            beyond_rows[4 * q + j] = lane_roll(row, NZ - 32 * j) if j else row

    def per_x(x, edge):
        beyond = beyond_rows[x]
        for y in range(NY):
            k = [jnp.broadcast_to(coef[i, x, y : y + 1, :], (S, NZ)) for i in range(7)]
            c = field[x, y]
            xm = xl[part * NY + y] if edge == "lo" else field[x - 1, y]
            xp = xh[part * NY + y] if edge == "hi" else field[x + 1, y]
            ym = field[x, y - 1] if y else yl[part * NX + x]
            yp = field[x, y + 1] if y < NY - 1 else yh[part * NX + x]
            ends = lane_roll(beyond, NZ - 2 - 2 * y)
            zm = jnp.where(first, ends, lane_roll(c, 1))
            zp = jnp.where(last, ends, lane_roll(c, NZ - 1))
            o = ((k[0] * c - k[1] * xm) - (k[2] * xp + k[3] * ym)) - ((k[4] * yp + k[5] * zm) + k[6] * zp)
            out[x, y] = o
            if emit:
                if edge == "lo":
                    oxl[y] = o
                if edge == "hi":
                    oxh[y] = o
                if y == 0:
                    oyl[x] = o
                if y == NY - 1:
                    oyh[x] = o

    per_x(0, "lo")
    lax.fori_loop(0, NX // 2 - 1, lambda j, c: (per_x(2 * j + 1, ""), per_x(2 * j + 2, ""), c)[2], 0)
    per_x(NX - 1, "hi")
    if emit:

        def ends_of(x):
            acc = jnp.zeros((S, NZ), F32)
            for y in range(NY):
                acc = pack_z(acc, out[x, y], y, lane)
            staged[x] = acc

        lax.fori_loop(0, NX // 4, lambda j, c: ([ends_of(4 * j + i) for i in range(4)], c)[1], 0)
        put_z_faces(ozf, 0, staged, lane)
    for src, dst in zip(others, faces):
        dst[src.shape[0] :] = src[...]


def stencil(field, halos, coef, part=0, emit=True, carry=(), after=()):
    shape = lambda n: jax.ShapeDtypeStruct((n, S, NZ), F32)
    sent = 2 if carry else 1
    faces = [shape(n * sent) for n in (16, 16, 16, 16, 4)] if emit else []
    out = pl.pallas_call(
        functools.partial(stencil_kernel, part, emit, bool(carry), len(after)),
        in_specs=[VMEM] * (8 + len(carry)) + [pl.BlockSpec(memory_space=pl.ANY)] * len(after),
        out_specs=[VMEM] * (1 + len(faces)),
        out_shape=[jax.ShapeDtypeStruct((NX, NY, S, NZ), F32)] + faces,
        scratch_shapes=[pltpu.VMEM((NX, S, NZ), F32)] * 2,
        compiler_params=grant(9),
        cost_estimate=pl.CostEstimate(flops=8 << 20, bytes_accessed=12 << 20, transcendentals=0),
        name=f"stencil_{part}_{len(faces)}_{len(carry)}",
    )(field, *halos, coef, *carry, *after)
    return out[0], tuple(out[1:])


def exchange(faces):
    xl, xh, yl, yh, zf = faces
    halos = []
    for axis, low, high in (("gx", xl, xh), ("gy", yl, yh), ("gz", zf, zf)):
        n = lax.axis_size(axis)
        halos.append(lax.ppermute(high, axis, [(j, (j + 1) % n) for j in range(n)]))
        halos.append(lax.ppermute(low, axis, [(j, (j - 1) % n) for j in range(n)]))
    return halos


def split(fields, halves, x):
    n = 16 * len(fields)
    for y in range(NY):
        row = x * NY + y
        for i, ref in enumerate(fields):
            v = ref[x, y]
            hi = v.astype(BF16)
            halves[row, 16 * i : 16 * i + 16, :] = hi
            halves[row, n + 16 * i : n + 16 * i + 16, :] = (v - hi.astype(F32)).astype(BF16)
    return side(halves, x)


def side(halves, x):
    return jnp.concatenate([halves[x * NY + y] for y in range(NY)], axis=1)


def nt(a, b):
    return lax.dot_general(a, b, (((1,), (1,)), ((), ())), preferred_element_type=F32)


def gram_first_kernel(d, q, r, halves, acc):
    def per_x(x, c):
        op = split((d, q, r), halves, x)
        acc[...] += nt(op, op)
        return c

    acc[...] = jnp.zeros_like(acc)
    lax.fori_loop(0, NX // 2, lambda j, c: per_x(2 * j + 1, per_x(2 * j, c)), 0)


def gram_second_kernel(w, z, before, first, halves, gram, acc):
    def per_x(x, c):
        op = split((w, z), halves, x)
        acc[...] += nt(jnp.concatenate([side(before, x), op], axis=0), op)
        return c

    acc[...] = jnp.zeros_like(acc)
    lax.fori_loop(0, NX // 2, lambda j, c: per_x(2 * j + 1, per_x(2 * j, c)), 0)
    pad = lambda m: jnp.concatenate([m, jnp.zeros((m.shape[0], 128 - m.shape[1]), F32)], axis=1)
    lane, lane2 = lanes((48, 128)), lanes((32, 128))
    a = pad(first[...])
    a = a[:48] + a[48:]
    a = jnp.where(lane < 48, a + lane_roll(a, 80), 0.0)
    b = pad(acc[...])
    top, low = b[:48] + b[48:96], b[96:128] + b[128:160]
    top = jnp.where(lane < 32, top + lane_roll(top, 96), 0.0)
    low = jnp.where(lane2 < 32, low + lane_roll(low, 96), 0.0)
    a = a + lane_roll(top, 48)
    gram[:32, :] = a[:32] + lane_roll(low, 80)
    gram[32:, :] = a[32:]


def gram_first(d, q, r):
    return pl.pallas_call(
        gram_first_kernel,
        in_specs=[VMEM] * 3,
        out_specs=[VMEM] * 2,
        out_shape=[jax.ShapeDtypeStruct((NX * NY, 96, NZ), BF16), jax.ShapeDtypeStruct((96, 96), F32)],
        compiler_params=grant(14),
        cost_estimate=pl.CostEstimate(flops=8 << 20, bytes_accessed=12 << 20, transcendentals=0),
        name="gram_first",
    )(d, q, r)


def gram_second(w, z, halves, first):
    return pl.pallas_call(
        gram_second_kernel,
        in_specs=[VMEM] * 4,
        out_specs=[VMEM] * 2,
        out_shape=[jax.ShapeDtypeStruct((NX * NY, 64, NZ), BF16), jax.ShapeDtypeStruct((48, 128), F32)],
        scratch_shapes=[pltpu.VMEM((160, 64), F32)],
        compiler_params=grant(18),
        name="gram_second",
    )(w, z, halves, first)


def add_kernel(*refs):
    total = refs[0][...]
    for ref in refs[1:-1]:
        total = total + ref[...]
    refs[-1][...] = total


def add(*parts):
    return pl.pallas_call(
        add_kernel,
        in_specs=[VMEM] * len(parts),
        out_specs=VMEM,
        out_shape=jax.ShapeDtypeStruct(parts[0].shape, F32),
        compiler_params=grant(1),
        name="add",
    )(*parts)


def gather_parts(part):
    gy, gz = lax.axis_size("gy"), lax.axis_size("gz")
    far = (gy // 2 * gz, gz // 2)
    stages = (("gz", (1,)), ("gy", range(1, gy // 2)), ("gx", range(1, lax.axis_size("gx"))))
    stages += ((("gy", "gz"), [far[0]] + [far[1], far[0] ^ far[1]] * (gz > 2)),)
    for axis, masks in stages:
        n = lax.axis_size(axis)
        parts = (part, *[lax.ppermute(part, axis, [(j, j ^ s) for j in range(n)]) for s in masks])
        part = add(*parts) if axis != ("gy", "gz") else parts
    return part


def rows128(m):
    return jnp.concatenate([m, jnp.zeros((128 - m.shape[0], 128), F32)], axis=0)


def mm(a, b):
    return jnp.dot(a, rows128(b), precision=lax.Precision.HIGHEST, preferred_element_type=F32)


def mm_nt(a, b):
    return lax.dot_general(
        a, rows128(b), (((1,), (1,)), ((), ())), precision=lax.Precision.HIGHEST, preferred_element_type=F32
    )


def eye_at(lane, sub, off):
    return jnp.where(lane == sub + off, 1.0, 0.0).astype(F32)


def two_rows(m, k):
    one, two = m[k : k + 1, :], m[k + 1 : k + 2, :]
    return one, two, one[:, k : k + 1], one[:, k + 1 : k + 2], two[:, k : k + 1], two[:, k + 1 : k + 2]


def spd_inverse(m, lane, sub):
    m = jnp.where(lane < 16, m, eye_at(lane, sub, 16))
    for k in range(0, S, 2):
        one, two, a, b, c, d = two_rows(m, k)
        inv = 1.0 / a
        ratio = c * inv
        two = (two - ratio * one) / (d - ratio * b)
        one = (one - b * two) * inv
        rest = m - m[:, k : k + 1] * one - m[:, k + 1 : k + 2] * two
        m = jnp.where(sub == k, one, jnp.where(sub == k + 1, two, rest))
    return jnp.where(lane < 16, lane_roll(m, 112), 0.0)


def factor_inverse(m, lane, sub):
    m = jnp.where(lane < 16, m, eye_at(lane, sub, 16))
    for k in range(0, S, 2):
        one, two, a, _, c, d = two_rows(m, k)
        scale = lax.rsqrt(a)
        one = one * scale
        low = c * scale
        scale2 = lax.rsqrt(d - low * low)
        two = (two - low * one) * scale2
        left = m[:, k : k + 1] * scale
        right = (m[:, k + 1 : k + 2] - left * low) * scale2
        rest = jnp.where(sub > k + 1, m - left * one - right * two, m)
        m = jnp.where(sub == k, one, jnp.where(sub == k + 1, two, rest))
    return jnp.where(lane < 16, lane_roll(m, 112), 0.0)


def step(g, lane, sub):
    gd, gq, gr = g[:16], g[16:32], g[32:48]
    low = lane < 16
    curvature = 0.5 * (lane_roll(gd, 112) + gq)
    inv = spd_inverse(curvature, lane, sub)
    s_t = mm(jnp.where(low, gr, 0.0), inv)
    qq = jnp.where(low, lane_roll(gq, 112), 0.0)
    rq = jnp.where(low, lane_roll(gr, 112), 0.0) - mm(s_t, qq)
    c_t = -mm(rq, inv)
    r_t = eye_at(lane, sub, 32) - lane_roll(s_t, 16)
    f_t = r_t + c_t
    ff = mm_nt(mm(f_t, g), f_t)
    ff = 0.5 * (ff + mm_nt(f_t, mm(f_t, g)))
    inv_factor = factor_inverse(ff, lane, sub)
    return s_t, r_t, mm(inv_factor, f_t)


def algebra_kernel(*refs):
    coef_ref = refs[-1]
    lane = lanes((S, 128))
    sub = lax.broadcasted_iota(jnp.int32, (S, 128), 0)
    lane48, lane32 = lanes((48, 128)), lanes((32, 128))
    total = refs[0][...]
    for ref in refs[1:-1]:
        total = total + ref[...]
    g = total * (1.0 / (64 * 128 * 512))
    g1 = jnp.where(lane48 < 48, g, 0.0)
    s_t, r_t, d_t = step(g1, lane, sub)
    q_t = (
        lane_roll(jnp.where(lane < 16, d_t, 0.0), 16)
        + lane_roll(jnp.where((lane >= 32) & (lane < 48), d_t, 0.0), 16)
        + lane_roll(jnp.where((lane >= 16) & (lane < 32), d_t, 0.0), 48)
    )
    t = jnp.concatenate([d_t, q_t, r_t], axis=0)
    half = jnp.where(lane48 < 48, 0.5 * g, jnp.where(lane48 < 80, g, 0.0))
    corner = lane_roll(0.5 * g[:32], 96)
    corner = jnp.where((lane32 >= 48) & (lane32 < 80), corner, 0.0)
    h = mm(t, jnp.concatenate([half, corner], axis=0))
    g2 = mm_nt(h, t) + mm_nt(t, h)
    s2_t, r2_t, d2_t = step(g2, lane, sub)
    final = mm(jnp.concatenate([s2_t, r2_t, d2_t], axis=0), t)
    final = jnp.concatenate([final[:16] + s_t, final[16:]], axis=0)
    hi = final.astype(BF16).astype(F32)
    for i, part in enumerate((hi, final - hi)):
        coef_ref[48 * i : 48 * i + 48, :128] = jnp.where(lane48 < 48, part, lane_roll(part, 48)).astype(BF16)
        coef_ref[48 * i : 48 * i + 48, 128:] = jnp.where(lane48 < 32, lane_roll(part, 80), 0.0).astype(BF16)


def algebra(*parts):
    return pl.pallas_call(
        algebra_kernel,
        in_specs=[VMEM] * len(parts),
        out_specs=VMEM,
        out_shape=jax.ShapeDtypeStruct((96, 256), BF16),
        compiler_params=grant(2),
        name="algebra",
    )(*parts)


def leave_kernel(coef, first, second, sol, xo, ro, do, x_buf, r_buf, d_buf, sems):
    left = coef[:, :160]
    outs = ((xo, x_buf), (ro, r_buf), (do, d_buf))
    flat = [buf.reshape(S * NX * NY, NZ) for _, buf in outs]
    inp = sol.reshape(S * NX * NY, NZ)

    def per_x(x):
        for y in range(0, NY, 2):
            row = x * NY + y
            pair = [jnp.concatenate([h[row], h[row + 1]], axis=1) for h in (first, second)]
            res = jnp.dot(left, jnp.concatenate(pair, axis=0), preferred_element_type=F32)
            res = res[:48] + res[48:]
            for j in range(2):
                v = res[:, j * NZ : (j + 1) * NZ]
                rows = pl.ds(row + j, S, stride=NX * NY)
                flat[0][rows, :] = inp[rows, :] + v[:16]
                flat[1][rows, :] = v[16:32]
                flat[2][rows, :] = v[32:48]

    copies = []
    for i in range(CHUNKS):
        lax.fori_loop(i * CHUNK // 2, (i + 1) * CHUNK // 2, lambda j, c: (per_x(2 * j), per_x(2 * j + 1), c)[2], 0)
        part = pl.ds(CHUNK * i, CHUNK)
        for k, (out, buf) in enumerate(outs):
            copies.append(pltpu.make_async_copy(buf.at[:, part], out.at[:, part], sems.at[k, i]))
            copies[-1].start()
    for copy in copies:
        copy.wait()


def leave(coef, first, second, sol):
    return pl.pallas_call(
        leave_kernel,
        in_specs=[VMEM] * 4,
        out_specs=[pl.BlockSpec(memory_space=pltpu.HBM)] * 3,
        out_shape=[jax.ShapeDtypeStruct((S, NX, NY, NZ), F32)] * 3,
        scratch_shapes=[pltpu.VMEM((S, NX, NY, NZ), F32)] * 3 + [pltpu.SemaphoreType.DMA((3, CHUNKS))],
        compiler_params=grant(24),
        name="leave",
    )(coef, first, second, sol)


def body(sol, residual, direction, kappa, cond):
    d, r, *faces = enter(direction, residual, cond)
    start = exchange(faces)
    coef = coefs(kappa, cond, start)
    ld, faces = stencil(d, start, coef)
    halos = exchange(faces)
    lr, lr_faces = stencil(r, start, coef, part=1)
    q, faces = stencil(ld, halos, coef, carry=lr_faces)
    both = exchange(faces)
    halves, gram = gram_first(d, q, r)
    lq, faces = stencil(q, both, coef, after=(gram,))
    halos = exchange(faces)
    w, _ = stencil(lr, both, coef, part=1, emit=False)
    z, _ = stencil(lq, halos, coef, emit=False)
    more, gram = gram_second(w, z, halves, gram)
    return tuple(leave(algebra(*gather_parts(gram)), halves, more, sol))


def solution(mesh):
    fields = P(None, *AXES)
    cells = P(*AXES)
    return jax.shard_map(
        body,
        mesh=mesh,
        in_specs=(fields, fields, fields, cells, cells),
        out_specs=(fields, fields, fields),
        check_vma=False,
    )
```

```python
import functools

import jax
import jax.numpy as jnp
from jax import lax
from jax.experimental import pallas as pl
from jax.experimental.pallas import tpu as pltpu
from jax.sharding import PartitionSpec as P

AXES = ("gx", "gy", "gz")
S = 16
NX, NY, NZ = 16, 16, 128
F32, BF16 = jnp.float32, jnp.bfloat16
VMEM = pl.BlockSpec(memory_space=pltpu.VMEM)


def grant(mib):
    return pltpu.CompilerParams(vmem_limit_bytes=mib << 20)


def lanes(shape):
    return lax.broadcasted_iota(jnp.int32, shape, len(shape) - 1)


def lane_roll(v, shift):
    return pltpu.roll(v, shift, v.ndim - 1)


def pack_z(acc, v, y, lane):
    return acc + lane_roll(jnp.where((lane == 0) | (lane == NZ - 1), v, 0.0), 2 * y + 1)


def put_z_faces(ref, base, staged, lane):
    for q in range(4):
        row = staged[4 * q]
        for j in range(1, 4):
            row = jnp.where(lane >= 32 * j, lane_roll(staged[4 * q + j], 32 * j), row)
        ref[base + q] = row


CHUNK = 4
CHUNKS = NX // CHUNK


def enter_kernel(d_ref, r_ref, c_ref, d_out, r_out, xl, xh, yl, yh, zf, d_in, r_in, c_in, staged, sems):
    lane = lanes((S, NZ))
    pairs = ((d_ref, d_in, d_out), (r_ref, r_in, r_out))
    cond_copy = pltpu.make_async_copy(c_ref, c_in, sems.at[2, 0])
    copies = [
        [
            pltpu.make_async_copy(src.at[:, pl.ds(CHUNK * i, CHUNK)], dst.at[:, pl.ds(CHUNK * i, CHUNK)], sems.at[f, i])
            for f, (src, dst, _) in enumerate(pairs)
        ]
        for i in range(CHUNKS)
    ]
    for group in copies:
        for copy in group:
            copy.start()
    cond_copy.start()

    def per_x(x):
        for f, (_, buf, out) in enumerate(pairs):
            flat = buf.reshape(S * NX * NY, NZ)
            acc = jnp.zeros((S, NZ), F32)
            for y in range(NY):
                v = flat[pl.ds(x * NY + y, S, stride=NX * NY), :]
                out[x, y] = v
                acc = pack_z(acc, v, y, lane)
                if y == 0:
                    yl[f * NX + x] = v
                if y == NY - 1:
                    yh[f * NX + x] = v
            staged[f, x] = acc

    for i, group in enumerate(copies):
        for copy in group:
            copy.wait()
        lax.fori_loop(i * CHUNK // 2, (i + 1) * CHUNK // 2, lambda j, c: (per_x(2 * j), per_x(2 * j + 1), c)[2], 0)
    cond_copy.wait()
    ends = jnp.zeros((S, NZ), F32)
    for x in range(NX):
        cond = c_in[x]
        yl[2 * NX, x : x + 1, :] = cond[0:1]
        yh[2 * NX, x : x + 1, :] = cond[NY - 1 : NY]
        ends = pack_z(ends, cond, x, lane)
    zf[8] = ends
    for f, (_, _, out) in enumerate(pairs):
        put_z_faces(zf, 4 * f, staged.at[f], lane)
        for y in range(NY):
            xl[f * NY + y] = out[0, y]
            xh[f * NY + y] = out[NX - 1, y]
    xl[2 * NY] = c_in[0]
    xh[2 * NY] = c_in[NX - 1]


def enter(direction, residual, conductance):
    shape = lambda n: jax.ShapeDtypeStruct((n, S, NZ), F32)
    rows = (33, 33, 33, 33, 9)
    return pl.pallas_call(
        enter_kernel,
        in_specs=[pl.BlockSpec(memory_space=pltpu.HBM)] * 3,
        out_specs=[VMEM] * 7,
        out_shape=[jax.ShapeDtypeStruct((NX, NY, S, NZ), F32)] * 2 + [shape(n) for n in rows],
        scratch_shapes=[pltpu.VMEM((S, NX, NY, NZ), F32)] * 2
        + [pltpu.VMEM((NX, NY, NZ), F32), pltpu.VMEM((2, NX, S, NZ), F32), pltpu.SemaphoreType.DMA((3, CHUNKS))],
        compiler_params=grant(12),
        name="enter",
    )(*[pltpu.with_memory_space_constraint(v, pltpu.HBM) for v in (direction, residual, conductance)])


def coef_kernel(kappa, cond, xl, xh, yl, yh, zl, zh, out):
    flag = []
    for axis in AXES:
        i, n = lax.axis_index(axis), lax.axis_size(axis)
        flag += [jnp.where(i > 0, 1.0, 0.0).astype(F32), jnp.where(i < n - 1, 1.0, 0.0).astype(F32)]
    lane = lanes((NY, NZ))
    sub = lax.broadcasted_iota(jnp.int32, (NY, NZ), 0)

    def per_x(x, _):
        c = cond[x]
        prev = jnp.where(x == 0, xl[2 * NY] * flag[0], cond[jnp.maximum(x - 1, 0)])
        nxt = jnp.where(x == NX - 1, xh[2 * NY] * flag[1], cond[jnp.minimum(x + 1, NX - 1)])
        ylo = yl[2 * NX, pl.ds(x, 1), :] * flag[2]
        yhi = yh[2 * NX, pl.ds(x, 1), :] * flag[3]
        ym = jnp.where(sub == 0, ylo, pltpu.roll(c, 1, 0))
        yp = jnp.where(sub == NY - 1, yhi, pltpu.roll(c, NY - 1, 0))
        zlo = lane_roll(zl[8], lax.rem(NZ - 2 * x, NZ)) * flag[4]
        zhi = lane_roll(zh[8], NZ - 2 - 2 * x) * flag[5]
        zm = jnp.where(lane == 0, zlo, lane_roll(c, 1))
        zp = jnp.where(lane == NZ - 1, zhi, lane_roll(c, NZ - 1))
        g = [0.5 * (c + n) for n in (prev, nxt, ym, yp, zm, zp)]
        out[0, x] = kappa[x] + ((g[0] + g[1]) + (g[2] + g[3]) + (g[4] + g[5]))
        out[1, x] = jnp.where(x == 0, g[0] * flag[0], g[0])
        out[2, x] = jnp.where(x == NX - 1, g[1] * flag[1], g[1])
        out[3, x] = jnp.where(sub == 0, g[2] * flag[2], g[2])
        out[4, x] = jnp.where(sub == NY - 1, g[3] * flag[3], g[3])
        out[5, x] = jnp.where(lane == 0, g[4] * flag[4], g[4])
        out[6, x] = jnp.where(lane == NZ - 1, g[5] * flag[5], g[5])
        return 0

    lax.fori_loop(0, NX, per_x, 0)


def coefs(kappa, cond, halos):
    return pl.pallas_call(
        coef_kernel,
        in_specs=[VMEM] * 8,
        out_specs=VMEM,
        out_shape=jax.ShapeDtypeStruct((7, NX, NY, NZ), F32),
        compiler_params=grant(4),
        name="coefs",
    )(kappa, cond, *halos)


def stencil_kernel(part, emit, carry, after, field, xl, xh, yl, yh, zl, zh, coef, *refs):
    lane = lanes((S, NZ))
    first, last = lane == 0, lane == NZ - 1
    even = lax.rem(lane, 2) == 0
    others, out, faces = refs[: 5 * carry], refs[5 * carry + after], refs[5 * carry + after + 1 :]
    beyond_rows, staged = refs[-2:]
    if emit:
        oxl, oxh, oyl, oyh, ozf = faces[:5]

    for q in range(4):
        row = jnp.where(even, lane_roll(zl[part * 4 + q], 2), zh[part * 4 + q])
        for j in range(4):
            beyond_rows[4 * q + j] = lane_roll(row, NZ - 32 * j) if j else row

    def per_x(x, edge):
        beyond = beyond_rows[x]
        for y in range(NY):
            k = [jnp.broadcast_to(coef[i, x, y : y + 1, :], (S, NZ)) for i in range(7)]
            c = field[x, y]
            xm = xl[part * NY + y] if edge == "lo" else field[x - 1, y]
            xp = xh[part * NY + y] if edge == "hi" else field[x + 1, y]
            ym = field[x, y - 1] if y else yl[part * NX + x]
            yp = field[x, y + 1] if y < NY - 1 else yh[part * NX + x]
            ends = lane_roll(beyond, NZ - 2 - 2 * y)
            zm = jnp.where(first, ends, lane_roll(c, 1))
            zp = jnp.where(last, ends, lane_roll(c, NZ - 1))
            o = ((k[0] * c - k[1] * xm) - (k[2] * xp + k[3] * ym)) - ((k[4] * yp + k[5] * zm) + k[6] * zp)
            out[x, y] = o
            if emit:
                if edge == "lo":
                    oxl[y] = o
                if edge == "hi":
                    oxh[y] = o
                if y == 0:
                    oyl[x] = o
                if y == NY - 1:
                    oyh[x] = o

    per_x(0, "lo")
    lax.fori_loop(0, NX // 2 - 1, lambda j, c: (per_x(2 * j + 1, ""), per_x(2 * j + 2, ""), c)[2], 0)
    per_x(NX - 1, "hi")
    if emit:

        def ends_of(x):
            acc = jnp.zeros((S, NZ), F32)
            for y in range(NY):
                acc = pack_z(acc, out[x, y], y, lane)
            staged[x] = acc

        lax.fori_loop(0, NX // 4, lambda j, c: ([ends_of(4 * j + i) for i in range(4)], c)[1], 0)
        put_z_faces(ozf, 0, staged, lane)
    for src, dst in zip(others, faces):
        dst[src.shape[0] :] = src[...]


def stencil(field, halos, coef, part=0, emit=True, carry=(), after=()):
    shape = lambda n: jax.ShapeDtypeStruct((n, S, NZ), F32)
    sent = 2 if carry else 1
    faces = [shape(n * sent) for n in (16, 16, 16, 16, 4)] if emit else []
    out = pl.pallas_call(
        functools.partial(stencil_kernel, part, emit, bool(carry), len(after)),
        in_specs=[VMEM] * (8 + len(carry)) + [pl.BlockSpec(memory_space=pl.ANY)] * len(after),
        out_specs=[VMEM] * (1 + len(faces)),
        out_shape=[jax.ShapeDtypeStruct((NX, NY, S, NZ), F32)] + faces,
        scratch_shapes=[pltpu.VMEM((NX, S, NZ), F32)] * 2,
        compiler_params=grant(9),
        cost_estimate=pl.CostEstimate(flops=8 << 20, bytes_accessed=12 << 20, transcendentals=0),
        name=f"stencil_{part}_{len(faces)}_{len(carry)}",
    )(field, *halos, coef, *carry, *after)
    return out[0], tuple(out[1:])


def exchange(faces):
    xl, xh, yl, yh, zf = faces
    halos = []
    for axis, low, high in (("gx", xl, xh), ("gy", yl, yh), ("gz", zf, zf)):
        n = lax.axis_size(axis)
        halos.append(lax.ppermute(high, axis, [(j, (j + 1) % n) for j in range(n)]))
        halos.append(lax.ppermute(low, axis, [(j, (j - 1) % n) for j in range(n)]))
    return halos


def split(fields, halves, x):
    n = 16 * len(fields)
    for y in range(NY):
        row = x * NY + y
        for i, ref in enumerate(fields):
            v = ref[x, y]
            hi = v.astype(BF16)
            halves[row, 16 * i : 16 * i + 16, :] = hi
            halves[row, n + 16 * i : n + 16 * i + 16, :] = (v - hi.astype(F32)).astype(BF16)
    return side(halves, x)


def side(halves, x):
    return jnp.concatenate([halves[x * NY + y] for y in range(NY)], axis=1)


def nt(a, b):
    return lax.dot_general(a, b, (((1,), (1,)), ((), ())), preferred_element_type=F32)


def gram_first_kernel(d, q, r, halves, acc):
    def per_x(x, c):
        op = split((d, q, r), halves, x)
        acc[...] += nt(op, op)
        return c

    acc[...] = jnp.zeros_like(acc)
    lax.fori_loop(0, NX // 2, lambda j, c: per_x(2 * j + 1, per_x(2 * j, c)), 0)


def gram_second_kernel(w, z, before, first, halves, gram, acc):
    def per_x(x, c):
        op = split((w, z), halves, x)
        acc[...] += nt(jnp.concatenate([side(before, x), op], axis=0), op)
        return c

    acc[...] = jnp.zeros_like(acc)
    lax.fori_loop(0, NX // 2, lambda j, c: per_x(2 * j + 1, per_x(2 * j, c)), 0)
    pad = lambda m: jnp.concatenate([m, jnp.zeros((m.shape[0], 128 - m.shape[1]), F32)], axis=1)
    lane, lane2 = lanes((48, 128)), lanes((32, 128))
    a = pad(first[...])
    a = a[:48] + a[48:]
    a = jnp.where(lane < 48, a + lane_roll(a, 80), 0.0)
    b = pad(acc[...])
    top, low = b[:48] + b[48:96], b[96:128] + b[128:160]
    top = jnp.where(lane < 32, top + lane_roll(top, 96), 0.0)
    low = jnp.where(lane2 < 32, low + lane_roll(low, 96), 0.0)
    a = a + lane_roll(top, 48)
    gram[:32, :] = a[:32] + lane_roll(low, 80)
    gram[32:, :] = a[32:]


def gram_first(d, q, r):
    return pl.pallas_call(
        gram_first_kernel,
        in_specs=[VMEM] * 3,
        out_specs=[VMEM] * 2,
        out_shape=[jax.ShapeDtypeStruct((NX * NY, 96, NZ), BF16), jax.ShapeDtypeStruct((96, 96), F32)],
        compiler_params=grant(14),
        cost_estimate=pl.CostEstimate(flops=8 << 20, bytes_accessed=12 << 20, transcendentals=0),
        name="gram_first",
    )(d, q, r)


def gram_second(w, z, halves, first):
    return pl.pallas_call(
        gram_second_kernel,
        in_specs=[VMEM] * 4,
        out_specs=[VMEM] * 2,
        out_shape=[jax.ShapeDtypeStruct((NX * NY, 64, NZ), BF16), jax.ShapeDtypeStruct((48, 128), F32)],
        scratch_shapes=[pltpu.VMEM((160, 64), F32)],
        compiler_params=grant(18),
        name="gram_second",
    )(w, z, halves, first)


def add_kernel(*refs):
    total = refs[0][...]
    for ref in refs[1:-1]:
        total = total + ref[...]
    refs[-1][...] = total


def add(*parts):
    return pl.pallas_call(
        add_kernel,
        in_specs=[VMEM] * len(parts),
        out_specs=VMEM,
        out_shape=jax.ShapeDtypeStruct(parts[0].shape, F32),
        compiler_params=grant(1),
        name="add",
    )(*parts)


def gather_parts(part):
    gy, gz = lax.axis_size("gy"), lax.axis_size("gz")
    far = (gy // 2 * gz, gz // 2)
    stages = (("gz", (1,)), ("gy", range(1, gy // 2)), ("gx", range(1, lax.axis_size("gx"))))
    stages += ((("gy", "gz"), [far[0]] + [far[1], far[0] ^ far[1]] * (gz > 2)),)
    for axis, masks in stages:
        n = lax.axis_size(axis)
        parts = (part, *[lax.ppermute(part, axis, [(j, j ^ s) for j in range(n)]) for s in masks])
        part = add(*parts) if axis != ("gy", "gz") else parts
    return part


def rows128(m):
    return jnp.concatenate([m, jnp.zeros((128 - m.shape[0], 128), F32)], axis=0)


def mm(a, b):
    return jnp.dot(a, rows128(b), precision=lax.Precision.HIGHEST, preferred_element_type=F32)


def mm_nt(a, b):
    return lax.dot_general(
        a, rows128(b), (((1,), (1,)), ((), ())), precision=lax.Precision.HIGHEST, preferred_element_type=F32
    )


def eye_at(lane, sub, off):
    return jnp.where(lane == sub + off, 1.0, 0.0).astype(F32)


def spd_inverse(m, lane, sub):
    m = jnp.where(lane < 16, m, eye_at(lane, sub, 16))
    for k in range(S):
        column = jnp.broadcast_to(m[:, k : k + 1], m.shape)
        row = m[k : k + 1, :] / column[k : k + 1, :]
        m = jnp.where(sub == k, row, m - column * row)
    return jnp.where(lane < 16, lane_roll(m, 112), 0.0)


def factor_inverse(m, lane, sub):
    m = jnp.where(lane < 16, m, eye_at(lane, sub, 16))
    for k in range(S):
        column = jnp.broadcast_to(m[:, k : k + 1], m.shape)
        scale = lax.rsqrt(column[k : k + 1, :])
        row = m[k : k + 1, :] * scale
        m = jnp.where(sub == k, row, jnp.where(sub > k, m - (column * scale) * row, m))
    return jnp.where(lane < 16, lane_roll(m, 112), 0.0)


def step(g, lane, sub):
    gd, gq, gr = g[:16], g[16:32], g[32:48]
    low = lane < 16
    curvature = 0.5 * (lane_roll(gd, 112) + gq)
    inv = spd_inverse(curvature, lane, sub)
    s_t = mm(jnp.where(low, gr, 0.0), inv)
    qq = jnp.where(low, lane_roll(gq, 112), 0.0)
    rq = jnp.where(low, lane_roll(gr, 112), 0.0) - mm(s_t, qq)
    c_t = -mm(rq, inv)
    r_t = eye_at(lane, sub, 32) - lane_roll(s_t, 16)
    f_t = r_t + c_t
    ff = mm_nt(mm(f_t, g), f_t)
    inv_factor = factor_inverse(ff, lane, sub)
    return s_t, r_t, mm(inv_factor, f_t)


def algebra_kernel(*refs):
    coef_ref = refs[-1]
    lane = lanes((S, 128))
    sub = lax.broadcasted_iota(jnp.int32, (S, 128), 0)
    lane48, lane32 = lanes((48, 128)), lanes((32, 128))
    total = refs[0][...]
    for ref in refs[1:-1]:
        total = total + ref[...]
    g = total * (1.0 / (64 * 128 * 512))
    g1 = jnp.where(lane48 < 48, g, 0.0)
    s_t, r_t, d_t = step(g1, lane, sub)
    q_t = (
        lane_roll(jnp.where(lane < 16, d_t, 0.0), 16)
        + lane_roll(jnp.where((lane >= 32) & (lane < 48), d_t, 0.0), 16)
        + lane_roll(jnp.where((lane >= 16) & (lane < 32), d_t, 0.0), 48)
    )
    t = jnp.concatenate([d_t, q_t, r_t], axis=0)
    half = jnp.where(lane48 < 48, 0.5 * g, jnp.where(lane48 < 80, g, 0.0))
    corner = lane_roll(0.5 * g[:32], 96)
    corner = jnp.where((lane32 >= 48) & (lane32 < 80), corner, 0.0)
    h = mm(t, jnp.concatenate([half, corner], axis=0))
    g2 = mm_nt(h, t) + mm_nt(t, h)
    s2_t, r2_t, d2_t = step(g2, lane, sub)
    final = mm(jnp.concatenate([s2_t, r2_t, d2_t], axis=0), t)
    final = jnp.concatenate([final[:16] + s_t, final[16:]], axis=0)
    hi = final.astype(BF16).astype(F32)
    for i, part in enumerate((hi, final - hi)):
        coef_ref[48 * i : 48 * i + 48, :128] = jnp.where(lane48 < 48, part, lane_roll(part, 48)).astype(BF16)
        coef_ref[48 * i : 48 * i + 48, 128:] = jnp.where(lane48 < 32, lane_roll(part, 80), 0.0).astype(BF16)


def algebra(*parts):
    return pl.pallas_call(
        algebra_kernel,
        in_specs=[VMEM] * len(parts),
        out_specs=VMEM,
        out_shape=jax.ShapeDtypeStruct((96, 256), BF16),
        compiler_params=grant(2),
        name="algebra",
    )(*parts)


def leave_kernel(coef, first, second, sol, xo, ro, do, x_buf, r_buf, d_buf, sems):
    left = coef[:, :160]
    outs = ((xo, x_buf), (ro, r_buf), (do, d_buf))
    flat = [buf.reshape(S * NX * NY, NZ) for _, buf in outs]
    inp = sol.reshape(S * NX * NY, NZ)

    def per_x(x):
        for y in range(0, NY, 2):
            row = x * NY + y
            pair = [jnp.concatenate([h[row], h[row + 1]], axis=1) for h in (first, second)]
            res = jnp.dot(left, jnp.concatenate(pair, axis=0), preferred_element_type=F32)
            res = res[:48] + res[48:]
            for j in range(2):
                v = res[:, j * NZ : (j + 1) * NZ]
                rows = pl.ds(row + j, S, stride=NX * NY)
                flat[0][rows, :] = inp[rows, :] + v[:16]
                flat[1][rows, :] = v[16:32]
                flat[2][rows, :] = v[32:48]

    copies = []
    for i in range(CHUNKS):
        lax.fori_loop(i * CHUNK // 2, (i + 1) * CHUNK // 2, lambda j, c: (per_x(2 * j), per_x(2 * j + 1), c)[2], 0)
        part = pl.ds(CHUNK * i, CHUNK)
        for k, (out, buf) in enumerate(outs):
            copies.append(pltpu.make_async_copy(buf.at[:, part], out.at[:, part], sems.at[k, i]))
            copies[-1].start()
    for copy in copies:
        copy.wait()


def leave(coef, first, second, sol):
    return pl.pallas_call(
        leave_kernel,
        in_specs=[VMEM] * 4,
        out_specs=[pl.BlockSpec(memory_space=pltpu.HBM)] * 3,
        out_shape=[jax.ShapeDtypeStruct((S, NX, NY, NZ), F32)] * 3,
        scratch_shapes=[pltpu.VMEM((S, NX, NY, NZ), F32)] * 3 + [pltpu.SemaphoreType.DMA((3, CHUNKS))],
        compiler_params=grant(24),
        name="leave",
    )(coef, first, second, sol)


def body(sol, residual, direction, kappa, cond):
    d, r, *faces = enter(direction, residual, cond)
    start = exchange(faces)
    coef = coefs(kappa, cond, start)
    ld, faces = stencil(d, start, coef)
    halos = exchange(faces)
    lr, lr_faces = stencil(r, start, coef, part=1)
    q, faces = stencil(ld, halos, coef, carry=lr_faces)
    both = exchange(faces)
    halves, gram = gram_first(d, q, r)
    lq, faces = stencil(q, both, coef, after=(gram,))
    halos = exchange(faces)
    w, _ = stencil(lr, both, coef, part=1, emit=False)
    z, _ = stencil(lq, halos, coef, emit=False)
    more, gram = gram_second(w, z, halves, gram)
    return tuple(leave(algebra(*gather_parts(gram)), halves, more, sol))


def solution(mesh):
    fields = P(None, *AXES)
    cells = P(*AXES)
    return jax.shard_map(
        body,
        mesh=mesh,
        in_specs=(fields, fields, fields, cells, cells),
        out_specs=(fields, fields, fields),
        check_vma=False,
    )
```

```python
import functools

import jax
import jax.numpy as jnp
from jax import lax
from jax.experimental import pallas as pl
from jax.experimental.pallas import tpu as pltpu
from jax.sharding import PartitionSpec as P

AXES = ("gx", "gy", "gz")
S = 16
NX, NY, NZ = 16, 16, 128
F32, BF16 = jnp.float32, jnp.bfloat16
VMEM = pl.BlockSpec(memory_space=pltpu.VMEM)


def grant(mib):
    return pltpu.CompilerParams(vmem_limit_bytes=mib << 20)


def lanes(shape):
    return lax.broadcasted_iota(jnp.int32, shape, len(shape) - 1)


def lane_roll(v, shift):
    return pltpu.roll(v, shift, v.ndim - 1)


def pack_z(acc, v, y, lane):
    return acc + lane_roll(jnp.where((lane == 0) | (lane == NZ - 1), v, 0.0), 2 * y + 1)


def put_z_faces(ref, base, staged, lane):
    for q in range(4):
        row = staged[4 * q]
        for j in range(1, 4):
            row = jnp.where(lane >= 32 * j, lane_roll(staged[4 * q + j], 32 * j), row)
        ref[base + q] = row


CHUNK = 4
CHUNKS = NX // CHUNK


def enter_kernel(d_ref, r_ref, c_ref, d_out, r_out, xl, xh, yl, yh, zf, d_in, r_in, c_in, staged, sems):
    lane = lanes((S, NZ))
    pairs = ((d_ref, d_in, d_out), (r_ref, r_in, r_out))
    cond_copy = pltpu.make_async_copy(c_ref, c_in, sems.at[2, 0])
    copies = [
        [
            pltpu.make_async_copy(src.at[:, pl.ds(CHUNK * i, CHUNK)], dst.at[:, pl.ds(CHUNK * i, CHUNK)], sems.at[f, i])
            for f, (src, dst, _) in enumerate(pairs)
        ]
        for i in range(CHUNKS)
    ]
    for group in copies:
        for copy in group:
            copy.start()
    cond_copy.start()

    def per_x(x):
        for f, (_, buf, out) in enumerate(pairs):
            flat = buf.reshape(S * NX * NY, NZ)
            acc = jnp.zeros((S, NZ), F32)
            for y in range(NY):
                v = flat[pl.ds(x * NY + y, S, stride=NX * NY), :]
                out[x, y] = v
                acc = pack_z(acc, v, y, lane)
                if y == 0:
                    yl[f * NX + x] = v
                if y == NY - 1:
                    yh[f * NX + x] = v
            staged[f, x] = acc

    for i, group in enumerate(copies):
        for copy in group:
            copy.wait()
        lax.fori_loop(i * CHUNK // 2, (i + 1) * CHUNK // 2, lambda j, c: (per_x(2 * j), per_x(2 * j + 1), c)[2], 0)
    cond_copy.wait()
    ends = jnp.zeros((S, NZ), F32)
    for x in range(NX):
        cond = c_in[x]
        yl[2 * NX, x : x + 1, :] = cond[0:1]
        yh[2 * NX, x : x + 1, :] = cond[NY - 1 : NY]
        ends = pack_z(ends, cond, x, lane)
    zf[8] = ends
    for f, (_, _, out) in enumerate(pairs):
        put_z_faces(zf, 4 * f, staged.at[f], lane)
        for y in range(NY):
            xl[f * NY + y] = out[0, y]
            xh[f * NY + y] = out[NX - 1, y]
    xl[2 * NY] = c_in[0]
    xh[2 * NY] = c_in[NX - 1]


def enter(direction, residual, conductance):
    shape = lambda n: jax.ShapeDtypeStruct((n, S, NZ), F32)
    rows = (33, 33, 33, 33, 9)
    return pl.pallas_call(
        enter_kernel,
        in_specs=[pl.BlockSpec(memory_space=pltpu.HBM)] * 3,
        out_specs=[VMEM] * 7,
        out_shape=[jax.ShapeDtypeStruct((NX, NY, S, NZ), F32)] * 2 + [shape(n) for n in rows],
        scratch_shapes=[pltpu.VMEM((S, NX, NY, NZ), F32)] * 2
        + [pltpu.VMEM((NX, NY, NZ), F32), pltpu.VMEM((2, NX, S, NZ), F32), pltpu.SemaphoreType.DMA((3, CHUNKS))],
        compiler_params=grant(12),
        name="enter",
    )(*[pltpu.with_memory_space_constraint(v, pltpu.HBM) for v in (direction, residual, conductance)])


def coef_kernel(kappa, cond, xl, xh, yl, yh, zl, zh, out):
    flag = []
    for axis in AXES:
        i, n = lax.axis_index(axis), lax.axis_size(axis)
        flag += [jnp.where(i > 0, 1.0, 0.0).astype(F32), jnp.where(i < n - 1, 1.0, 0.0).astype(F32)]
    lane = lanes((NY, NZ))
    sub = lax.broadcasted_iota(jnp.int32, (NY, NZ), 0)

    def per_x(x, _):
        c = cond[x]
        prev = jnp.where(x == 0, xl[2 * NY] * flag[0], cond[jnp.maximum(x - 1, 0)])
        nxt = jnp.where(x == NX - 1, xh[2 * NY] * flag[1], cond[jnp.minimum(x + 1, NX - 1)])
        ylo = yl[2 * NX, pl.ds(x, 1), :] * flag[2]
        yhi = yh[2 * NX, pl.ds(x, 1), :] * flag[3]
        ym = jnp.where(sub == 0, ylo, pltpu.roll(c, 1, 0))
        yp = jnp.where(sub == NY - 1, yhi, pltpu.roll(c, NY - 1, 0))
        zlo = lane_roll(zl[8], lax.rem(NZ - 2 * x, NZ)) * flag[4]
        zhi = lane_roll(zh[8], NZ - 2 - 2 * x) * flag[5]
        zm = jnp.where(lane == 0, zlo, lane_roll(c, 1))
        zp = jnp.where(lane == NZ - 1, zhi, lane_roll(c, NZ - 1))
        g = [0.5 * (c + n) for n in (prev, nxt, ym, yp, zm, zp)]
        out[0, x] = kappa[x] + ((g[0] + g[1]) + (g[2] + g[3]) + (g[4] + g[5]))
        out[1, x] = jnp.where(x == 0, g[0] * flag[0], g[0])
        out[2, x] = jnp.where(x == NX - 1, g[1] * flag[1], g[1])
        out[3, x] = jnp.where(sub == 0, g[2] * flag[2], g[2])
        out[4, x] = jnp.where(sub == NY - 1, g[3] * flag[3], g[3])
        out[5, x] = jnp.where(lane == 0, g[4] * flag[4], g[4])
        out[6, x] = jnp.where(lane == NZ - 1, g[5] * flag[5], g[5])
        return 0

    lax.fori_loop(0, NX, per_x, 0)


def coefs(kappa, cond, halos):
    return pl.pallas_call(
        coef_kernel,
        in_specs=[VMEM] * 8,
        out_specs=VMEM,
        out_shape=jax.ShapeDtypeStruct((7, NX, NY, NZ), F32),
        compiler_params=grant(4),
        name="coefs",
    )(kappa, cond, *halos)


def stencil_kernel(part, emit, carry, after, field, xl, xh, yl, yh, zl, zh, coef, *refs):
    lane = lanes((S, NZ))
    first, last = lane == 0, lane == NZ - 1
    even = lax.rem(lane, 2) == 0
    others, out, faces = refs[: 5 * carry], refs[5 * carry + after], refs[5 * carry + after + 1 :]
    beyond_rows, staged = refs[-2:]
    if emit:
        oxl, oxh, oyl, oyh, ozf = faces[:5]

    for q in range(4):
        row = jnp.where(even, lane_roll(zl[part * 4 + q], 2), zh[part * 4 + q])
        for j in range(4):
            beyond_rows[4 * q + j] = lane_roll(row, NZ - 32 * j) if j else row

    def per_x(x, edge):
        beyond = beyond_rows[x]
        for y in range(NY):
            k = [jnp.broadcast_to(coef[i, x, y : y + 1, :], (S, NZ)) for i in range(7)]
            c = field[x, y]
            xm = xl[part * NY + y] if edge == "lo" else field[x - 1, y]
            xp = xh[part * NY + y] if edge == "hi" else field[x + 1, y]
            ym = field[x, y - 1] if y else yl[part * NX + x]
            yp = field[x, y + 1] if y < NY - 1 else yh[part * NX + x]
            ends = lane_roll(beyond, NZ - 2 - 2 * y)
            zm = jnp.where(first, ends, lane_roll(c, 1))
            zp = jnp.where(last, ends, lane_roll(c, NZ - 1))
            o = ((k[0] * c - k[1] * xm) - (k[2] * xp + k[3] * ym)) - ((k[4] * yp + k[5] * zm) + k[6] * zp)
            out[x, y] = o
            if emit:
                if edge == "lo":
                    oxl[y] = o
                if edge == "hi":
                    oxh[y] = o
                if y == 0:
                    oyl[x] = o
                if y == NY - 1:
                    oyh[x] = o

    per_x(0, "lo")
    lax.fori_loop(0, NX // 2 - 1, lambda j, c: (per_x(2 * j + 1, ""), per_x(2 * j + 2, ""), c)[2], 0)
    per_x(NX - 1, "hi")
    if emit:

        def ends_of(x):
            acc = jnp.zeros((S, NZ), F32)
            for y in range(NY):
                acc = pack_z(acc, out[x, y], y, lane)
            staged[x] = acc

        lax.fori_loop(0, NX // 4, lambda j, c: ([ends_of(4 * j + i) for i in range(4)], c)[1], 0)
        put_z_faces(ozf, 0, staged, lane)
    for src, dst in zip(others, faces):
        dst[src.shape[0] :] = src[...]


def stencil(field, halos, coef, part=0, emit=True, carry=(), after=()):
    shape = lambda n: jax.ShapeDtypeStruct((n, S, NZ), F32)
    sent = 2 if carry else 1
    faces = [shape(n * sent) for n in (16, 16, 16, 16, 4)] if emit else []
    out = pl.pallas_call(
        functools.partial(stencil_kernel, part, emit, bool(carry), len(after)),
        in_specs=[VMEM] * (8 + len(carry)) + [pl.BlockSpec(memory_space=pl.ANY)] * len(after),
        out_specs=[VMEM] * (1 + len(faces)),
        out_shape=[jax.ShapeDtypeStruct((NX, NY, S, NZ), F32)] + faces,
        scratch_shapes=[pltpu.VMEM((NX, S, NZ), F32)] * 2,
        compiler_params=grant(9),
        cost_estimate=pl.CostEstimate(flops=8 << 20, bytes_accessed=12 << 20, transcendentals=0),
        name=f"stencil_{part}_{len(faces)}_{len(carry)}",
    )(field, *halos, coef, *carry, *after)
    return out[0], tuple(out[1:])


def exchange(faces):
    xl, xh, yl, yh, zf = faces
    halos = []
    for axis, low, high in (("gx", xl, xh), ("gy", yl, yh), ("gz", zf, zf)):
        n = lax.axis_size(axis)
        halos.append(lax.ppermute(high, axis, [(j, (j + 1) % n) for j in range(n)]))
        halos.append(lax.ppermute(low, axis, [(j, (j - 1) % n) for j in range(n)]))
    return halos


def split(fields, halves, x):
    n = 16 * len(fields)
    for y in range(NY):
        row = x * NY + y
        for i, ref in enumerate(fields):
            v = ref[x, y]
            hi = v.astype(BF16)
            halves[row, 16 * i : 16 * i + 16, :] = hi
            halves[row, n + 16 * i : n + 16 * i + 16, :] = (v - hi.astype(F32)).astype(BF16)
    return side(halves, x)


def side(halves, x):
    return jnp.concatenate([halves[x * NY + y] for y in range(NY)], axis=1)


def nt(a, b):
    return lax.dot_general(a, b, (((1,), (1,)), ((), ())), preferred_element_type=F32)


def gram_first_kernel(d, q, r, halves, acc):
    def per_x(x, c):
        op = split((d, q, r), halves, x)
        acc[...] += nt(op, op)
        return c

    acc[...] = jnp.zeros_like(acc)
    lax.fori_loop(0, NX // 2, lambda j, c: per_x(2 * j + 1, per_x(2 * j, c)), 0)


def gram_second_kernel(w, z, before, first, halves, gram, acc):
    def per_x(x, c):
        op = split((w, z), halves, x)
        acc[...] += nt(jnp.concatenate([side(before, x), op], axis=0), op)
        return c

    acc[...] = jnp.zeros_like(acc)
    lax.fori_loop(0, NX // 2, lambda j, c: per_x(2 * j + 1, per_x(2 * j, c)), 0)
    pad = lambda m: jnp.concatenate([m, jnp.zeros((m.shape[0], 128 - m.shape[1]), F32)], axis=1)
    lane, lane2 = lanes((48, 128)), lanes((32, 128))
    a = pad(first[...])
    a = a[:48] + a[48:]
    a = jnp.where(lane < 48, a + lane_roll(a, 80), 0.0)
    b = pad(acc[...])
    top, low = b[:48] + b[48:96], b[96:128] + b[128:160]
    top = jnp.where(lane < 32, top + lane_roll(top, 96), 0.0)
    low = jnp.where(lane2 < 32, low + lane_roll(low, 96), 0.0)
    a = a + lane_roll(top, 48)
    gram[:32, :] = a[:32] + lane_roll(low, 80)
    gram[32:, :] = a[32:]


def gram_first(d, q, r):
    return pl.pallas_call(
        gram_first_kernel,
        in_specs=[VMEM] * 3,
        out_specs=[VMEM] * 2,
        out_shape=[jax.ShapeDtypeStruct((NX * NY, 96, NZ), BF16), jax.ShapeDtypeStruct((96, 96), F32)],
        compiler_params=grant(14),
        cost_estimate=pl.CostEstimate(flops=8 << 20, bytes_accessed=12 << 20, transcendentals=0),
        name="gram_first",
    )(d, q, r)


def gram_second(w, z, halves, first):
    return pl.pallas_call(
        gram_second_kernel,
        in_specs=[VMEM] * 4,
        out_specs=[VMEM] * 2,
        out_shape=[jax.ShapeDtypeStruct((NX * NY, 64, NZ), BF16), jax.ShapeDtypeStruct((48, 128), F32)],
        scratch_shapes=[pltpu.VMEM((160, 64), F32)],
        compiler_params=grant(18),
        name="gram_second",
    )(w, z, halves, first)


def add_kernel(*refs):
    total = refs[0][...]
    for ref in refs[1:-1]:
        total = total + ref[...]
    refs[-1][...] = total


def add(*parts):
    return pl.pallas_call(
        add_kernel,
        in_specs=[VMEM] * len(parts),
        out_specs=VMEM,
        out_shape=jax.ShapeDtypeStruct(parts[0].shape, F32),
        compiler_params=grant(1),
        name="add",
    )(*parts)


def gather_parts(part):
    gy, gz = lax.axis_size("gy"), lax.axis_size("gz")
    far = (gy // 2 * gz, gz // 2)
    stages = (("gz", (1,)), ("gy", range(1, gy // 2)), ("gx", range(1, lax.axis_size("gx"))))
    stages += ((("gy", "gz"), [far[0]] + [far[1], far[0] ^ far[1]] * (gz > 2)),)
    for axis, masks in stages:
        n = lax.axis_size(axis)
        parts = (part, *[lax.ppermute(part, axis, [(j, j ^ s) for j in range(n)]) for s in masks])
        part = add(*parts) if axis != ("gy", "gz") else parts
    return part


def rows128(m):
    return jnp.concatenate([m, jnp.zeros((128 - m.shape[0], 128), F32)], axis=0)


def mm(a, b):
    return jnp.dot(a, rows128(b), precision=lax.Precision.HIGHEST, preferred_element_type=F32)


def mm_nt(a, b):
    return lax.dot_general(
        a, rows128(b), (((1,), (1,)), ((), ())), precision=lax.Precision.HIGHEST, preferred_element_type=F32
    )


def eye_at(lane, sub, off):
    return jnp.where(lane == sub + off, 1.0, 0.0).astype(F32)


def columns_of(m):
    return [jnp.broadcast_to(m[:, j : j + 1], m.shape) for j in range(S)]


def spd_inverse(m, lane, sub):
    m = jnp.where(lane < 16, m, eye_at(lane, sub, 16))
    cols = columns_of(m)
    for k in range(S):
        col = cols[k]
        inv = 1.0 / col[k : k + 1, :]
        for j in range(k + 1, S):
            lead = cols[j][k : k + 1, :] * inv
            cols[j] = jnp.where(sub == k, lead, cols[j] - col * lead)
        row = m[k : k + 1, :] * inv
        m = jnp.where(sub == k, row, m - col * row)
    return jnp.where(lane < 16, lane_roll(m, 112), 0.0)


def factor_inverse(m, lane, sub):
    m = jnp.where(lane < 16, m, eye_at(lane, sub, 16))
    cols = columns_of(m)
    for k in range(S):
        scale = lax.rsqrt(cols[k][k : k + 1, :])
        col = cols[k] * scale
        for j in range(k + 1, S):
            cols[j] = cols[j] - col * (cols[j][k : k + 1, :] * scale)
        row = m[k : k + 1, :] * scale
        m = jnp.where(sub == k, row, jnp.where(sub > k, m - col * row, m))
    return jnp.where(lane < 16, lane_roll(m, 112), 0.0)


def step(g, lane, sub):
    gd, gq, gr = g[:16], g[16:32], g[32:48]
    low = lane < 16
    curvature = 0.5 * (lane_roll(gd, 112) + gq)
    inv = spd_inverse(curvature, lane, sub)
    s_t = mm(jnp.where(low, gr, 0.0), inv)
    qq = jnp.where(low, lane_roll(gq, 112), 0.0)
    rq = jnp.where(low, lane_roll(gr, 112), 0.0) - mm(s_t, qq)
    c_t = -mm(rq, inv)
    r_t = eye_at(lane, sub, 32) - lane_roll(s_t, 16)
    f_t = r_t + c_t
    ff = mm_nt(mm(f_t, g), f_t)
    inv_factor = factor_inverse(ff, lane, sub)
    return s_t, r_t, mm(inv_factor, f_t)


def algebra_kernel(*refs):
    coef_ref = refs[-1]
    lane = lanes((S, 128))
    sub = lax.broadcasted_iota(jnp.int32, (S, 128), 0)
    lane48, lane32 = lanes((48, 128)), lanes((32, 128))
    total = refs[0][...]
    for ref in refs[1:-1]:
        total = total + ref[...]
    g = total * (1.0 / (64 * 128 * 512))
    g1 = jnp.where(lane48 < 48, g, 0.0)
    s_t, r_t, d_t = step(g1, lane, sub)
    q_t = (
        lane_roll(jnp.where(lane < 16, d_t, 0.0), 16)
        + lane_roll(jnp.where((lane >= 32) & (lane < 48), d_t, 0.0), 16)
        + lane_roll(jnp.where((lane >= 16) & (lane < 32), d_t, 0.0), 48)
    )
    t = jnp.concatenate([d_t, q_t, r_t], axis=0)
    half = jnp.where(lane48 < 48, 0.5 * g, jnp.where(lane48 < 80, g, 0.0))
    corner = lane_roll(0.5 * g[:32], 96)
    corner = jnp.where((lane32 >= 48) & (lane32 < 80), corner, 0.0)
    h = mm(t, jnp.concatenate([half, corner], axis=0))
    g2 = mm_nt(h, t) + mm_nt(t, h)
    s2_t, r2_t, d2_t = step(g2, lane, sub)
    final = mm(jnp.concatenate([s2_t, r2_t, d2_t], axis=0), t)
    final = jnp.concatenate([final[:16] + s_t, final[16:]], axis=0)
    hi = final.astype(BF16).astype(F32)
    for i, part in enumerate((hi, final - hi)):
        coef_ref[48 * i : 48 * i + 48, :128] = jnp.where(lane48 < 48, part, lane_roll(part, 48)).astype(BF16)
        coef_ref[48 * i : 48 * i + 48, 128:] = jnp.where(lane48 < 32, lane_roll(part, 80), 0.0).astype(BF16)


def algebra(*parts):
    return pl.pallas_call(
        algebra_kernel,
        in_specs=[VMEM] * len(parts),
        out_specs=VMEM,
        out_shape=jax.ShapeDtypeStruct((96, 256), BF16),
        compiler_params=grant(2),
        name="algebra",
    )(*parts)


def leave_kernel(coef, first, second, sol, xo, ro, do, x_buf, r_buf, d_buf, sems):
    left = coef[:, :160]
    outs = ((xo, x_buf), (ro, r_buf), (do, d_buf))
    flat = [buf.reshape(S * NX * NY, NZ) for _, buf in outs]
    inp = sol.reshape(S * NX * NY, NZ)

    def per_x(x):
        for y in range(0, NY, 2):
            row = x * NY + y
            pair = [jnp.concatenate([h[row], h[row + 1]], axis=1) for h in (first, second)]
            res = jnp.dot(left, jnp.concatenate(pair, axis=0), preferred_element_type=F32)
            res = res[:48] + res[48:]
            for j in range(2):
                v = res[:, j * NZ : (j + 1) * NZ]
                rows = pl.ds(row + j, S, stride=NX * NY)
                flat[0][rows, :] = inp[rows, :] + v[:16]
                flat[1][rows, :] = v[16:32]
                flat[2][rows, :] = v[32:48]

    copies = []
    for i in range(CHUNKS):
        lax.fori_loop(i * CHUNK // 2, (i + 1) * CHUNK // 2, lambda j, c: (per_x(2 * j), per_x(2 * j + 1), c)[2], 0)
        part = pl.ds(CHUNK * i, CHUNK)
        for k, (out, buf) in enumerate(outs):
            copies.append(pltpu.make_async_copy(buf.at[:, part], out.at[:, part], sems.at[k, i]))
            copies[-1].start()
    for copy in copies:
        copy.wait()


def leave(coef, first, second, sol):
    return pl.pallas_call(
        leave_kernel,
        in_specs=[VMEM] * 4,
        out_specs=[pl.BlockSpec(memory_space=pltpu.HBM)] * 3,
        out_shape=[jax.ShapeDtypeStruct((S, NX, NY, NZ), F32)] * 3,
        scratch_shapes=[pltpu.VMEM((S, NX, NY, NZ), F32)] * 3 + [pltpu.SemaphoreType.DMA((3, CHUNKS))],
        compiler_params=grant(24),
        name="leave",
    )(coef, first, second, sol)


def body(sol, residual, direction, kappa, cond):
    d, r, *faces = enter(direction, residual, cond)
    start = exchange(faces)
    coef = coefs(kappa, cond, start)
    ld, faces = stencil(d, start, coef)
    halos = exchange(faces)
    lr, lr_faces = stencil(r, start, coef, part=1)
    q, faces = stencil(ld, halos, coef, carry=lr_faces)
    both = exchange(faces)
    halves, gram = gram_first(d, q, r)
    lq, faces = stencil(q, both, coef, after=(gram,))
    halos = exchange(faces)
    w, _ = stencil(lr, both, coef, part=1, emit=False)
    z, _ = stencil(lq, halos, coef, emit=False)
    more, gram = gram_second(w, z, halves, gram)
    return tuple(leave(algebra(*gather_parts(gram)), halves, more, sol))


def solution(mesh):
    fields = P(None, *AXES)
    cells = P(*AXES)
    return jax.shard_map(
        body,
        mesh=mesh,
        in_specs=(fields, fields, fields, cells, cells),
        out_specs=(fields, fields, fields),
        check_vma=False,
    )
```
